768 devices in a mesh: stream: 24 (over x, z_lo, core), girth: 32 (over z_hi, y).
Axes of the slice: x: 4, y: 8, z: 12 (z_hi: 4, z_lo: 3; z = z_hi * 3 + z_lo), core: 2. Of those that a mesh axis runs over, the one named last changes fastest.
Arguments:
- velocity: float32 [3, 768, 512, 128], P(None, 'stream', 'girth'), may hold values from -6 to 6
- pressure: float32 [768, 512, 128], P('stream', 'girth'), may hold values from -6 to 6
- turb_k: float32 [768, 512, 128], P('stream', 'girth'), may hold values from 0.05 to 0.5
- turb_omega: float32 [768, 512, 128], P('stream', 'girth'), may hold values from 0.5 to 5
- face_code: int32 [24, 32, 2], P('stream', 'girth'), may hold values from 0 to 1, as said below
- disc_cells: int32 [24, 16384], P('stream', 'girth'), may hold values from 0 to 65535
- disc_sector: int32 [24, 16384, 1], P('stream', 'girth'), may hold values from 0 to 31, as said below
- disc_weight: float32 [24, 16384], P('stream', 'girth'), may hold values from 0.2 to 2
Outputs:
- velocity_out: float32 [3, 768, 512, 128], P(None, 'stream', 'girth')
- pressure_out: float32 [768, 512, 128], P('stream', 'girth')
The draws below stay inside these ranges and needn't reach their ends.
Inputs may be any that keep to these rules, and one draw needn't show every extreme that they name: face_code[s, g, 1] equals face_code[s, (g + 1) mod 32, 0]. `disc_sector`: the 512 disc cells of one block name any one sector at most 32 times, and every block names some sector exactly 32 times. In some rows of blocks a sector is named by no block of the row.
All inputs are finite; a program needn't handle non-finite values.
Results may differ from the reference program's by a relative error of at most 0.000073.
Values sent between devices are 32-bit elements; how exact they have to be, the bound alone decides.
No kernel may reach another device: no remote copies, remote signals or barrier semaphores. Data moves between devices by JAX's collectives and lax.ppermute only.
A program may use at most 64 MiB of HBM per device.

```python
import math
import jax
import jax.numpy as jnp

BI = 32
BJ = 16
BK = 128
DMAX = 512
STREAM_BLOCKS = 24
GIRTH_BLOCKS = 32
CAP = 32
NI = 768
NJ = 512


def draw_face_code(key, part):
    upper_code = jax.random.randint(jax.random.fold_in(key, 11), (STREAM_BLOCKS, GIRTH_BLOCKS), 0, 2, dtype=jnp.int32)
    lower_code = jnp.roll(upper_code, 1, axis=1)
    return jnp.stack([lower_code, upper_code], axis=-1)


def draw_disc_sector(key, part):
    slot_count = 2 * DMAX
    slot_unit = slot_count * 2 ** 14
    slot_index = jnp.arange(slot_count, dtype=jnp.int32)
    slot_sector = slot_index // CAP
    base_noise = jax.random.randint(jax.random.fold_in(key, 21), (STREAM_BLOCKS, GIRTH_BLOCKS, slot_count), 0, 2 ** 14, dtype=jnp.int32)
    liking = jax.random.randint(jax.random.fold_in(key, 22), (STREAM_BLOCKS, 1, GIRTH_BLOCKS), 0, 4, dtype=jnp.int32)
    missing = jax.random.randint(jax.random.fold_in(key, 23), (STREAM_BLOCKS,), 0, GIRTH_BLOCKS, dtype=jnp.int32)
    flagged = jax.random.randint(jax.random.fold_in(key, 24), (STREAM_BLOCKS,), 0, 2, dtype=jnp.int32)
    first_row = jax.random.randint(jax.random.fold_in(key, 25), (), 0, STREAM_BLOCKS, dtype=jnp.int32)
    other_row = (first_row + 1 + jax.random.randint(jax.random.fold_in(key, 26), (), 0, STREAM_BLOCKS - 1, dtype=jnp.int32)) % STREAM_BLOCKS
    row_ids = jnp.arange(STREAM_BLOCKS, dtype=jnp.int32)
    flagged = jnp.where(row_ids == first_row, 1, jnp.where(row_ids == other_row, 0, flagged))
    hot_sector = (missing[:, None] + 1 + jax.random.randint(jax.random.fold_in(key, 27), (STREAM_BLOCKS, GIRTH_BLOCKS), 0, GIRTH_BLOCKS - 1, dtype=jnp.int32)) % GIRTH_BLOCKS
    liked = liking[:, :, slot_sector]
    is_hot = (slot_sector[None, None, :] == hot_sector[:, :, None]).astype(jnp.int32)
    is_missing = ((flagged[:, None, None] == 1) & (slot_sector[None, None, :] == missing[:, None, None])).astype(jnp.int32)
    score = base_noise * slot_count + slot_index[None, None, :] - liked * slot_unit - 16 * slot_unit * is_hot + 16 * slot_unit * is_missing
    chosen = jnp.argsort(score, axis=-1)[..., :DMAX]
    sectors = (chosen // CAP).astype(jnp.int32)
    order_noise = jax.random.randint(jax.random.fold_in(key, 28), (STREAM_BLOCKS, GIRTH_BLOCKS, DMAX), 0, 2 ** 14, dtype=jnp.int32) * DMAX + jnp.arange(DMAX, dtype=jnp.int32)[None, None, :]
    reorder = jnp.argsort(order_noise, axis=-1)
    sectors = jnp.take_along_axis(sectors, reorder, axis=-1)
    return sectors.reshape(STREAM_BLOCKS, GIRTH_BLOCKS * DMAX, 1)


def place_ends(result, stream_key, smallest, largest):
    extent = result.shape
    spot = [jax.random.randint(jax.random.fold_in(stream_key, axis), (), 0, extent[axis]) for axis in range(len(extent))]
    result = result.at[tuple(spot)].set(smallest)
    longest = extent.index(max(extent))
    spot[longest] = (spot[longest] + 1) % extent[longest]
    return result.at[tuple(spot)].set(largest)


def shard_levels(rng, extent, pieces, least, largest):
    factor_of = 1.0
    for dim, blocks in pieces:
        steps = jax.random.uniform(jax.random.fold_in(jax.random.fold_in(rng, 6), dim), (blocks,), jnp.float32, least / len(pieces), largest / len(pieces))
        factor_of = factor_of * jnp.repeat(jnp.exp(steps), extent[dim] // blocks).reshape((-1,) + (1,) * (len(extent) - 1 - dim))
    return factor_of


def gaussian(key, dims, scale, bound, shards=(), kind=jnp.bfloat16):
    result = jax.random.normal(key, dims, jnp.float32) * scale
    if len(shards) > 0:
        result = shard_levels(key, dims, shards, -0.22, 0.18) * result
    return jnp.clip(result, min=-bound, max=bound).astype(kind)


def setup_inputs(seed: int = 0) -> dict:
    seeds = jax.random.split(jax.random.key(seed), 9)
    velocity = gaussian(seeds[0], (3, NI, NJ, BK), 1.0, 6.0, ((1, 24), (2, 32)), jnp.float32)
    pressure = gaussian(seeds[1], (NI, NJ, BK), 1.0, 6.0, ((0, 24), (1, 32)), jnp.float32)
    turb_k = jnp.clip(jnp.exp(math.log(0.5) - 2.3025851 * jax.random.uniform(seeds[2], (NI, NJ, BK), jnp.float32) ** shard_levels(seeds[2], (NI, NJ, BK), ((0, 24), (1, 32)), -0.2, 0.2)), 0.05, 0.5)
    turb_omega = jnp.clip(jnp.exp(math.log(5.0) - 2.3025851 * jax.random.uniform(seeds[3], (NI, NJ, BK), jnp.float32) ** shard_levels(seeds[3], (NI, NJ, BK), ((0, 24), (1, 32)), -0.2, 0.2)), 0.5, 5.0)
    face_code = draw_face_code(jax.random.fold_in(seeds[8], 71), 0)
    disc_cells = place_ends(jax.random.randint(seeds[5], (STREAM_BLOCKS, GIRTH_BLOCKS * DMAX), 0, BI * BJ * BK), jax.random.fold_in(seeds[5], 1), 0, (BI * BJ * BK) - 1).astype(jnp.int32)
    disc_sector = draw_disc_sector(jax.random.fold_in(seeds[8], 71), 0)
    disc_weight = jnp.clip(jnp.exp(math.log(2.0) - 2.3025851 * jax.random.uniform(seeds[7], (STREAM_BLOCKS, GIRTH_BLOCKS * DMAX), jnp.float32) ** shard_levels(seeds[7], (STREAM_BLOCKS, GIRTH_BLOCKS * DMAX), ((0, 24), (1, 32)), -0.2, 0.2)), 0.2, 2.0)
    return {"velocity": velocity, "pressure": pressure, "turb_k": turb_k, "turb_omega": turb_omega, "face_code": face_code, "disc_cells": disc_cells, "disc_sector": disc_sector, "disc_weight": disc_weight}


time_step = 0.5
viscosity = 0.02
advect = 0.25
thrust = 8.0
target_speed = 0.5


def edge_values(values, like):
    return jnp.array(values, like.dtype).reshape(-1, 1, 1, 1)


def neighbours(fields, inlet_value, outlet_value, wall_sign, high_mask, low_mask):
    stream_low = jnp.concatenate([inlet_value * fields[:, :1], fields[:, :-1]], axis=1)
    stream_high = jnp.concatenate([fields[:, 1:], outlet_value * fields[:, -1:]], axis=1)
    forward = jnp.roll(fields, -1, axis=2)
    girth_high = jnp.where(high_mask, forward[..., ::-1], forward)
    backward = jnp.roll(fields, 1, axis=2)
    girth_low = jnp.where(low_mask, backward[..., ::-1], backward)
    normal_low = jnp.concatenate([wall_sign * fields[..., :1], fields[..., :-1]], axis=3)
    normal_high = jnp.concatenate([fields[..., 1:], jnp.zeros_like(fields[..., :1])], axis=3)
    return (stream_low, stream_high), (girth_low, girth_high), (normal_low, normal_high)


def spread(sides):
    return sides[0][0] + sides[0][1] + sides[1][0] + sides[1][1] + sides[2][0] + sides[2][1]


def reference(velocity, pressure, turb_k, turb_omega, face_code, disc_cells, disc_sector, disc_weight):
    row_block = jnp.arange(NI, dtype=jnp.int32) // BI
    column = jnp.arange(NJ, dtype=jnp.int32)
    col_block = column // BJ
    high_code = face_code[:, :, 1][row_block][:, col_block]
    low_code = face_code[:, :, 0][row_block][:, col_block]
    high_mask = ((column % BJ == BJ - 1)[None, :] & (high_code == 1))[None, :, :, None]
    low_mask = ((column % BJ == 0)[None, :] & (low_code == 1))[None, :, :, None]

    cell_index = disc_cells.reshape(STREAM_BLOCKS, GIRTH_BLOCKS, DMAX)
    local_i = cell_index // (BJ * BK)
    local_j = (cell_index // BK) % BJ
    local_k = cell_index % BK
    global_i = jnp.arange(STREAM_BLOCKS, dtype=jnp.int32)[:, None, None] * BI + local_i
    global_j = jnp.arange(GIRTH_BLOCKS, dtype=jnp.int32)[None, :, None] * BJ + local_j
    inflow = velocity[0][global_i, global_j, local_k]
    sector = disc_sector.reshape(STREAM_BLOCKS, GIRTH_BLOCKS, DMAX)
    sector_hot = (sector[..., None] == jnp.arange(GIRTH_BLOCKS, dtype=jnp.int32)).astype(velocity.dtype)
    summed = jnp.sum(sector_hot * inflow[..., None], axis=(1, 2))
    filled = jnp.sum(sector_hot, axis=(1, 2))
    sector_load = thrust * (target_speed - summed / jnp.maximum(filled, 1.0))
    cell_load = jnp.sum(sector_hot * sector_load[:, None, None, :], axis=-1)
    cell_load = cell_load * disc_weight.reshape(STREAM_BLOCKS, GIRTH_BLOCKS, DMAX)
    forcing = jnp.zeros((NI, NJ, BK), velocity.dtype).at[global_i, global_j, local_k].add(cell_load)

    effective = viscosity + turb_k / turb_omega
    speed_in = edge_values([0.0, 0.0, 0.0], velocity)
    speed_out = edge_values([1.0, 1.0, 1.0], velocity)
    speed_wall = edge_values([-1.0, -1.0, -1.0], velocity)
    press_in = edge_values([1.0], velocity)
    press_out = edge_values([0.0], velocity)
    press_wall = edge_values([1.0], velocity)

    sides = neighbours(velocity, speed_in, speed_out, speed_wall, high_mask, low_mask)
    press_sides = neighbours(pressure[None], press_in, press_out, press_wall, high_mask, low_mask)
    gradient = jnp.concatenate([press_sides[0][1] - press_sides[0][0], press_sides[1][1] - press_sides[1][0], press_sides[2][1] - press_sides[2][0]], axis=0)
    push = jnp.concatenate([forcing[None], jnp.zeros_like(velocity[1:])], axis=0)
    u_star = (velocity - time_step * advect * (sides[0][1] - sides[0][0]) + time_step * effective * spread(sides) - 0.5 * time_step * gradient + time_step * push) / (1.0 + 6.0 * time_step * effective)

    star_sides = neighbours(u_star, speed_in, speed_out, speed_wall, high_mask, low_mask)
    outflow = 0.5 * ((star_sides[0][1][0] - star_sides[0][0][0]) + (star_sides[1][1][1] - star_sides[1][0][1]) + (star_sides[2][1][2] - star_sides[2][0][2]))
    first_sweep = -outflow / (6.0 * time_step)
    first_sides = neighbours(first_sweep[None], press_in, press_out, press_wall, high_mask, low_mask)
    second_sweep = (spread(first_sides)[0] - outflow / time_step) / 6.0
    second_sides = neighbours(second_sweep[None], press_in, press_out, press_wall, high_mask, low_mask)
    correction = jnp.concatenate([second_sides[0][1] - second_sides[0][0], second_sides[1][1] - second_sides[1][0], second_sides[2][1] - second_sides[2][0]], axis=0)
    velocity_out = u_star - 0.5 * time_step * correction
    pressure_out = pressure + second_sweep
    return velocity_out, pressure_out
```

```python
import jax
import jax.numpy as jnp
from jax import lax
from jax.experimental import pallas as pl
from jax.experimental.pallas import tpu as pltpu
from jax.sharding import PartitionSpec as P

viscosity = 0.02
thrust = 8.0
target_speed = 0.5

BI, BJ, BK, DMAX = 32, 16, 128, 512
CELLS = BI * BJ
COLS = (3, 4, 3, 4, 3)
COL_AT = (0, 3, 7, 10, 14)
LAYERS = (4, 3, 3, 4, 3)
LAYER_AT = (0, 4, 7, 10, 14)
LIST_ROWS = 12
G_LIST = 17 * BI
G_ROWS = G_LIST + 16
WIDE = BJ + 8
S_LIST = 17 * WIDE
S_LOAD = S_LIST + 3 * LIST_ROWS
S_FACE = S_LOAD + 1
S_ROWS = S_LIST + 40
EL, EC = BI + 8, 48
LO, LO_OUT, LO_IN, OWN, HI_IN, HI_OUT, HI = 10, 14, 15, 16, 32, 33, 34
F32, BF16, I32 = jnp.float32, jnp.bfloat16, jnp.int32


def iota(shape, dim):
    return lax.broadcasted_iota(I32, shape, dim)


def three(x):
    a = x.astype(BF16)
    rest = x - a.astype(F32)
    b = rest.astype(BF16)
    c = (rest - b.astype(F32)).astype(BF16)
    return a, b, c


def wide_row(ref, at):
    return jnp.concatenate([ref[at + q : at + q + 1, :] for q in range(4)], axis=1)


def put_row(ref, at, row):
    for q in range(4):
        ref[at + q : at + q + 1, :] = row[:, q * BK : (q + 1) * BK]


def head_kernel(vel, prs, tk, tw, cells, sector, weight, sums, to_high, to_low):
    def column(f, j):
        rows = pl.ds(j, BI, stride=BJ)
        if f < 3:
            return vel[f, rows, :]
        if f == 3:
            return prs[rows, :]
        return viscosity + tk[rows, :] / tw[rows, :]

    for f in range(5):
        n = COLS[f]
        for c in range(n):
            at = (COL_AT[f] + c) * BI
            to_high[at : at + BI, :] = column(f, BJ - n + c)
            to_low[at : at + BI, :] = column(f, c)
    cell = cells[...]
    owner = sector[...]
    for ref in (to_high, to_low):
        put_row(ref, G_LIST, cell.astype(F32))
        put_row(ref, G_LIST + 4, owner.astype(F32))
        put_row(ref, G_LIST + 8, weight[...])
        ref[G_LIST + LIST_ROWS : G_ROWS, :] = jnp.zeros((4, BK), F32)
    pick = jnp.where(iota((CELLS, DMAX), 0) == cell // BK, 1.0, 0.0).astype(BF16)
    parts = jnp.concatenate(three(vel[0]), axis=1)
    found = lax.dot_general(parts, pick, (((0,), (0,)), ((), ())), preferred_element_type=F32)
    found = found[:BK] + found[BK : 2 * BK] + found[2 * BK :]
    inflow = jnp.sum(jnp.where(iota((BK, DMAX), 0) == cell % BK, found, 0.0), axis=0, keepdims=True)
    mine = iota((64, DMAX), 0)
    both = jnp.where(mine == owner, inflow, 0.0) + jnp.where(mine == owner + 32, 1.0, 0.0)
    both = jnp.concatenate([both, jnp.zeros((64, DMAX), F32)], axis=0)
    total = lax.dot_general(
        jnp.ones((8, DMAX), F32),
        both,
        (((1,), (1,)), ((), ())),
        precision=lax.Precision.HIGHEST,
        preferred_element_type=F32,
    )
    for t in range(sums.shape[0] // 8):
        sums[t * 8 : t * 8 + 8, :] = total


def middle_kernel(vel, prs, tk, tw, cells, sector, weight, face, from_low, from_high, sums, up, down, load):
    for f in range(5):
        n, m = LAYERS[f], COLS[f]
        for q in range(n):
            for ref, i in ((up, BI - n + q), (down, q)):
                at = (LAYER_AT[f] + q) * WIDE
                rows = pl.ds(i * BJ, BJ)
                if f < 3:
                    own = vel[f, rows, :]
                elif f == 3:
                    own = prs[rows, :]
                else:
                    own = viscosity + tk[rows, :] / tw[rows, :]
                ref[at : at + BJ, :] = own
                for c in range(m):
                    row = (COL_AT[f] + c) * BI + i
                    low_at, high_at = at + BJ + 4 - m + c, at + BJ + 4 + c
                    ref[low_at : low_at + 1, :] = from_low[row : row + 1, :]
                    ref[high_at : high_at + 1, :] = from_high[row : row + 1, :]
    total = jnp.sum(sums[...], axis=0, keepdims=True)
    filled = pltpu.roll(jnp.broadcast_to(total, (8, BK)), BK - 32, 1)[:1]
    value = thrust * (target_speed - total / jnp.maximum(filled, 1.0))
    value = jnp.where(iota((1, BK), 1) < 32, value, 0.0)
    load[...] = jnp.broadcast_to(value, (8, BK))
    lane = iota((1, BK), 1)
    sides = jnp.where(lane == 0, face[0], jnp.where(lane == 1, face[1], 0)).astype(F32)
    for ref in (up, down):
        put_row(ref, S_LIST, cells[...].astype(F32))
        put_row(ref, S_LIST + 4, sector[...].astype(F32))
        put_row(ref, S_LIST + 8, weight[...])
        ref[S_LIST + 12 : S_LIST + 24, :] = from_low[G_LIST : G_LIST + 12, :]
        ref[S_LIST + 24 : S_LIST + 36, :] = from_high[G_LIST : G_LIST + 12, :]
        ref[S_LOAD : S_LOAD + 1, :] = value
        ref[S_FACE : S_FACE + 1, :] = sides
        ref[S_FACE + 1 : S_ROWS, :] = jnp.zeros((S_ROWS - S_FACE - 1, BK), F32)


def spread_list(cell, owner, weight, load, row, count):
    mine = jnp.where(iota((BK, DMAX), 0) == owner, 1.0, 0.0)
    given = jnp.dot(load, mine, precision=lax.Precision.HIGHEST, preferred_element_type=F32)[:1] * weight
    value = jnp.where(iota((BK, DMAX), 0) == cell % BK, given, 0.0)
    parts = jnp.concatenate(three(value), axis=0)
    pick = jnp.where(iota((count, DMAX), 0) == row, 1.0, 0.0).astype(BF16)
    out = lax.dot_general(pick, parts, (((1,), (1,)), ((), ())), preferred_element_type=F32)
    return out[:, :BK] + out[:, BK : 2 * BK] + out[:, 2 * BK :]


def tail_kernel(vel, prs, tk, tw, cells, sector, weight, face, place, from_low, from_high, from_up, from_down, load, vel_out, prs_out, *scratch):
    block = scratch[:5]
    star = scratch[5:8]
    force, sweep, second = scratch[8:11]
    first_row = place[0] == 0
    last_row = place[0] == place[1] - 1

    def flat(ref):
        return ref.reshape(EL * EC, BK)

    for f in range(5):
        to = block[f]
        if f < 3:
            own = vel[f]
        elif f == 3:
            own = prs[...]
        else:
            own = viscosity + tk[...] / tw[...]
        to[4 : 4 + BI, OWN : OWN + BJ, :] = own.reshape(BI, BJ, BK)
        m, n = COLS[f], LAYERS[f]
        lines = flat(to)
        for c in range(m):
            at = (COL_AT[f] + c) * BI
            lines[pl.ds(4 * EC + LO + 4 - m + c, BI, stride=EC), :] = from_low[at : at + BI, :]
            lines[pl.ds(4 * EC + HI + c, BI, stride=EC), :] = from_high[at : at + BI, :]
        for q in range(n):
            at = (LAYER_AT[f] + q) * WIDE
            for ref, layer in ((from_up, 4 - n + q), (from_down, 4 + BI + q)):
                to[layer, OWN : OWN + BJ, :] = ref[at : at + BJ, :]
                to[layer, LO : LO + 4, :] = ref[at + BJ : at + BJ + 4, :]
                to[layer, HI : HI + 4, :] = ref[at + BJ + 4 : at + BJ + 8, :]

    layer = iota((EL, BK), 0)
    up_face = from_up[S_FACE : S_FACE + 1, :]
    down_face = from_down[S_FACE : S_FACE + 1, :]

    def turned(side):
        own = face[side].astype(F32)
        above = jnp.broadcast_to(up_face[:, side : side + 1], (EL, BK))
        below = jnp.broadcast_to(down_face[:, side : side + 1], (EL, BK))
        return jnp.where(layer < 4, above, jnp.where(layer < 4 + BI, own, below)) > 0.5

    low_turned, high_turned = turned(0), turned(1)
    backward = BK - 1 - iota((EL, BK), 1)

    def images(ref, outer=True):
        lines = flat(ref)
        for source, target, mask in (
            (LO + 3, LO_IN, low_turned),
            (HI, HI_IN, high_turned),
            (OWN, LO_OUT, low_turned),
            (OWN + BJ - 1, HI_OUT, high_turned),
        )[: 4 if outer else 2]:
            value = lines[pl.ds(source, EL, stride=EC), :]
            mirror = jnp.take_along_axis(value, backward, axis=1, mode="promise_in_bounds")
            lines[pl.ds(target, EL, stride=EC), :] = jnp.where(mask, mirror, value)

    @pl.when(first_row)
    def _():
        for f in range(3):
            block[f][3] = jnp.zeros((EC, BK), F32)
        block[3][3] = block[3][4]

    @pl.when(last_row)
    def _():
        for f in range(3):
            block[f][4 + BI] = block[f][3 + BI]
        block[3][4 + BI] = jnp.zeros((EC, BK), F32)

    for f in range(4):
        images(block[f])

    own_load = load[...]
    lists = {}
    lists[0, 0] = (cells[...], sector[...], weight[...], own_load)
    for d, ref in ((-1, from_low), (1, from_high)):
        lists[0, d] = tuple(wide_row(ref, G_LIST + 4 * q) for q in range(3)) + (own_load,)
    for s, ref in ((-1, from_up), (1, from_down)):
        there = jnp.broadcast_to(ref[S_LOAD : S_LOAD + 1, :], (8, BK))
        for n, d in enumerate((0, -1, 1)):
            at = S_LIST + LIST_ROWS * n
            lists[s, d] = tuple(wide_row(ref, at + 4 * q) for q in range(3)) + (there,)
    lines = flat(force)
    for (s, d), (cell, owner, share, there) in lists.items():
        cell, owner = cell.astype(I32), owner.astype(I32)
        i, j = cell // (BJ * BK), (cell // BK) % BJ
        depth = {-1: BI - 3, 0: 0, 1: 0}[s]
        if s == 0 and d == 0:
            out = spread_list(cell, owner, share, there, cell // BK, CELLS)
            force[4 : 4 + BI, OWN : OWN + BJ, :] = out.reshape(BI, BJ, BK)
        elif s == 0:
            j0 = BJ - 2 if d < 0 else 0
            row = jnp.where((j >= j0) & (j < j0 + 2), (j - j0) * BI + i, -1)
            out = spread_list(cell, owner, share, there, row, 2 * BI)
            for c in range(2):
                at = 4 * EC + (LO + 2 if d < 0 else HI) + c
                lines[pl.ds(at, BI, stride=EC), :] = out[c * BI : (c + 1) * BI]
        elif d == 0:
            row = jnp.where((i >= depth) & (i < depth + 3), (i - depth) * BJ + j, -1)
            out = spread_list(cell, owner, share, there, row, 3 * BJ)
            at = 1 if s < 0 else 4 + BI
            force[at : at + 3, OWN : OWN + BJ, :] = out.reshape(3, BJ, BK)
        else:
            i0 = BI - 2 if s < 0 else 0
            j0 = BJ - 2 if d < 0 else 0
            row = jnp.where((i >= i0) & (i < i0 + 2) & (j >= j0) & (j < j0 + 2), (i - i0) * 2 + (j - j0), -1)
            out = spread_list(cell, owner, share, there, row, 8)
            at = 2 if s < 0 else 4 + BI
            to = LO + 2 if d < 0 else HI
            for q in range(2):
                force[at + q, to : to + 2, :] = out[2 * q : 2 * q + 2]

    lane = iota((32, BK), 1)

    def below(x, sign):
        return jnp.where(lane[: x.shape[0]] == 0, sign * x, pltpu.roll(x, 1, 1))

    def above(x):
        return jnp.where(lane[: x.shape[0]] == BK - 1, 0.0, pltpu.roll(x, BK - 1, 1))

    mid, left, right = slice(8, 40), slice(7, 39), slice(9, 41)

    def star_step(l, carry):
        e = block[4][l, mid, :]
        share = 1.0 / (1.0 + 3.0 * e)
        half = 0.5 * e
        p = block[3]
        q = p[l, mid, :]
        slope = (
            p[l + 1, mid, :] - p[l - 1, mid, :],
            p[l, right, :] - p[l, left, :],
            above(q) - below(q, 1.0),
        )
        for c in range(3):
            u = block[c]
            x, a, b = u[l, mid, :], u[l - 1, mid, :], u[l + 1, mid, :]
            around = a + b + u[l, left, :] + u[l, right, :] + below(x, -1.0) + above(x)
            value = x - 0.125 * (b - a) + half * around - 0.25 * slope[c]
            if c == 0:
                value = value + 0.5 * force[l, mid, :]
            star[c][l, mid, :] = value * share
        return carry

    lax.fori_loop(1, EL - 1, star_step, 0)

    @pl.when(first_row)
    def _():
        star[0][3] = jnp.zeros((EC, BK), F32)

    @pl.when(last_row)
    def _():
        star[0][4 + BI] = star[0][3 + BI]

    images(star[1])

    def sweep_step(l, carry):
        x = star[2][l, mid, :]
        total = (star[0][l + 1, mid, :] - star[0][l - 1, mid, :]) + (star[1][l, right, :] - star[1][l, left, :])
        sweep[l, mid, :] = (total + (above(x) - below(x, -1.0))) * (-1.0 / 6.0)
        return carry

    lax.fori_loop(2, EL - 2, sweep_step, 0)

    @pl.when(first_row)
    def _():
        sweep[3] = sweep[4]

    @pl.when(last_row)
    def _():
        sweep[4 + BI] = jnp.zeros((EC, BK), F32)

    images(sweep)

    def second_step(l, carry):
        x = sweep[l, mid, :]
        around = sweep[l - 1, mid, :] + sweep[l + 1, mid, :] + sweep[l, left, :] + sweep[l, right, :]
        second[l, mid, :] = (around + below(x, 1.0) + above(x)) * (1.0 / 6.0) + x
        return carry

    lax.fori_loop(3, EL - 3, second_step, 0)

    @pl.when(first_row)
    def _():
        second[3] = second[4]

    @pl.when(last_row)
    def _():
        second[4 + BI] = jnp.zeros((EC, BK), F32)

    images(second, outer=False)
    own, own_left, own_right = slice(OWN, OWN + BJ), slice(OWN - 1, OWN + BJ - 1), slice(OWN + 1, OWN + BJ + 1)

    def out_step(i, carry):
        l = i + 4
        x = second[l, own, :]
        slope = (
            second[l + 1, own, :] - second[l - 1, own, :],
            second[l, own_right, :] - second[l, own_left, :],
            above(x) - below(x, 1.0),
        )
        for c in range(3):
            vel_out[c, i] = star[c][l, own, :] - 0.25 * slope[c]
        prs_out[i] = block[3][l, own, :] + x
        return carry

    lax.fori_loop(0, BI, out_step, 0)


def body(velocity, pressure, turb_k, turb_omega, face_code, disc_cells, disc_sector, disc_weight):
    streams, girths = lax.axis_size("stream"), lax.axis_size("girth")
    vmem = pl.BlockSpec(memory_space=pltpu.VMEM)
    smem = pl.BlockSpec(memory_space=pltpu.SMEM)
    params = pltpu.CompilerParams(vmem_limit_bytes=48 * 2**20)
    vel = velocity.reshape(3, CELLS, BK)
    prs, tk, tw = (x.reshape(CELLS, BK) for x in (pressure, turb_k, turb_omega))
    cells, sector, weight = disc_cells, disc_sector.reshape(1, DMAX), disc_weight
    face = face_code.reshape(2)
    place = jnp.stack([lax.axis_index("stream").astype(I32), jnp.int32(streams)])
    fields = (vel, prs, tk, tw, cells, sector, weight)

    g_pack = jax.ShapeDtypeStruct((G_ROWS, BK), F32)
    sums, to_high, to_low = pl.pallas_call(
        head_kernel,
        out_shape=(jax.ShapeDtypeStruct((girths, BK), F32), g_pack, g_pack),
        in_specs=[vmem] * 7,
        out_specs=(vmem,) * 3,
        compiler_params=params,
        name="head",
    )(*fields)
    ring = [(g, (g + 1) % girths) for g in range(girths)]
    from_low = lax.ppermute(to_high, "girth", ring)
    from_high = lax.ppermute(to_low, "girth", [(b, a) for a, b in ring])
    sums = lax.all_to_all(sums, "girth", split_axis=0, concat_axis=0, tiled=True)

    s_pack = jax.ShapeDtypeStruct((S_ROWS, BK), F32)
    up, down, load = pl.pallas_call(
        middle_kernel,
        out_shape=(s_pack, s_pack, jax.ShapeDtypeStruct((8, BK), F32)),
        in_specs=[vmem] * 7 + [smem] + [vmem] * 3,
        out_specs=(vmem,) * 3,
        compiler_params=params,
        name="middle",
    )(*fields, face, from_low, from_high, sums)
    chain = [(s, s + 1) for s in range(streams - 1)]
    from_up = lax.ppermute(up, "stream", chain)
    from_down = lax.ppermute(down, "stream", [(b, a) for a, b in chain])

    return pl.pallas_call(
        tail_kernel,
        out_shape=(
            jax.ShapeDtypeStruct((3, BI, BJ, BK), F32),
            jax.ShapeDtypeStruct((BI, BJ, BK), F32),
        ),
        in_specs=[vmem] * 7 + [smem] * 2 + [vmem] * 5,
        out_specs=(vmem,) * 2,
        scratch_shapes=[pltpu.VMEM((EL, EC, BK), F32)] * 11,
        compiler_params=params,
        name="tail",
    )(*fields, face, place, from_low, from_high, from_up, from_down, load)


def solution(mesh):
    block = P("stream", "girth", None)
    placed = (P(None, "stream", "girth", None), block, block, block, block, P("stream", "girth"), block, P("stream", "girth"))
    return jax.shard_map(
        body,
        mesh=mesh,
        in_specs=placed,
        out_specs=(P(None, "stream", "girth", None), block),
        check_vma=False,
    )
```

```python
import jax
import jax.numpy as jnp
from jax import lax
from jax.experimental import pallas as pl
from jax.experimental.pallas import tpu as pltpu
from jax.sharding import PartitionSpec as P

viscosity = 0.02
thrust = 8.0
target_speed = 0.5

BI, BJ, BK, DMAX = 32, 16, 128, 512
CELLS = BI * BJ
COLS = (3, 4, 3, 4, 3)
COL_AT = (0, 3, 7, 10, 14)
LAYERS = (4, 3, 3, 4, 3)
LAYER_AT = (0, 4, 7, 10, 14)
LIST_ROWS = 12
G_LIST = 17 * BI
G_ROWS = G_LIST + 16
WIDE = BJ + 8
FORCE_AT = 17
S_FACE = 20 * WIDE
S_ROWS = S_FACE + 8
INNER = (8, 32)
EL, EC = BI + 8, 48
LO, LO_OUT, LO_IN, OWN, HI_IN, HI_OUT, HI = 10, 14, 15, 16, 32, 33, 34
F32, BF16, I32 = jnp.float32, jnp.bfloat16, jnp.int32


def iota(shape, dim):
    return lax.broadcasted_iota(I32, shape, dim)


def three(x):
    a = x.astype(BF16)
    rest = x - a.astype(F32)
    b = rest.astype(BF16)
    c = (rest - b.astype(F32)).astype(BF16)
    return a, b, c


def wide_row(ref, at):
    return jnp.concatenate([ref[at + q : at + q + 1, :] for q in range(4)], axis=1)


def lines(ref):
    return ref.reshape(EL * EC, BK)


def put_row(ref, at, row):
    for q in range(4):
        ref[at + q : at + q + 1, :] = row[:, q * BK : (q + 1) * BK]


def head_kernel(vel, prs, tk, tw, cells, sector, weight, face, *refs):
    block, (sums, to_high, to_low, info) = refs[:5], refs[5:9]
    k_buf, w_buf, cell_buf, owner_buf, share_buf, face_buf, sem = refs[9:]
    inside = (slice(4, 4 + BI), slice(OWN, OWN + BJ))
    pairs = (
        (cells, cell_buf),
        (sector, owner_buf),
        (weight, share_buf),
        (face, face_buf),
        (vel.at[0], block[0].at[inside]),
        (vel.at[1], block[1].at[inside]),
        (vel.at[2], block[2].at[inside]),
        (prs, block[3].at[inside]),
        (tk, k_buf),
        (tw, w_buf),
    )
    copies = [pltpu.make_async_copy(a, b, sem.at[n]) for n, (a, b) in enumerate(pairs)]
    for copy in copies:
        copy.start()
    for copy in copies[:4]:
        copy.wait()
    cell, owner, share = cell_buf[...], owner_buf[...], share_buf[...]
    for ref in (to_high, to_low):
        put_row(ref, G_LIST, cell.astype(F32))
        put_row(ref, G_LIST + 4, owner.astype(F32))
        put_row(ref, G_LIST + 8, share)
        ref[G_LIST + LIST_ROWS : G_ROWS, :] = jnp.zeros((4, BK), F32)
    row = iota((8, BK), 0)
    sides = jnp.where(row == 0, face_buf[0, 0, 0], jnp.where(row == 1, face_buf[0, 0, 1], 0))
    info[...] = sides.astype(F32)
    pick = jnp.where(iota((CELLS, DMAX), 0) == cell // BK, 1.0, 0.0).astype(BF16)
    mine = iota((64, DMAX), 0)
    copies[4].wait()
    parts = jnp.concatenate(three(block[0][inside].reshape(CELLS, BK)), axis=1)
    found = lax.dot_general(parts, pick, (((0,), (0,)), ((), ())), preferred_element_type=F32)
    found = found[:BK] + found[BK : 2 * BK] + found[2 * BK :]
    inflow = jnp.sum(jnp.where(iota((BK, DMAX), 0) == cell % BK, found, 0.0), axis=0, keepdims=True)
    both = jnp.where(mine == owner, inflow, 0.0) + jnp.where(mine == owner + 32, 1.0, 0.0)
    both = jnp.concatenate([both, jnp.zeros((64, DMAX), F32)], axis=0)
    total = lax.dot_general(
        jnp.ones((8, DMAX), F32),
        both,
        (((1,), (1,)), ((), ())),
        precision=lax.Precision.HIGHEST,
        preferred_element_type=F32,
    )
    for t in range(sums.shape[0] // 8):
        sums[t * 8 : t * 8 + 8, :] = total
    for f in range(5):
        if f == 4:
            copies[8].wait()
            copies[9].wait()
            block[4][inside] = viscosity + k_buf[...] / w_buf[...]
        elif f:
            copies[4 + f].wait()
        flat = lines(block[f])
        n = COLS[f]
        for c in range(n):
            at = (COL_AT[f] + c) * BI
            to_high[at : at + BI, :] = flat[pl.ds(4 * EC + OWN + BJ - n + c, BI, stride=EC), :]
            to_low[at : at + BI, :] = flat[pl.ds(4 * EC + OWN + c, BI, stride=EC), :]


def listed(own, from_low, from_high):
    rows = [
        jnp.concatenate([wide_row(ref, G_LIST + 4 * q) for ref in (own, from_low, from_high)], axis=1)
        for q in range(3)
    ]
    return rows[0].astype(I32), rows[1].astype(I32), rows[2]


def list_load(owner, share, load):
    mine = jnp.where(iota((BK, owner.shape[1]), 0) == owner, 1.0, 0.0)
    given = jnp.dot(load, mine, precision=lax.Precision.HIGHEST, preferred_element_type=F32)
    return given[:1] * share


def spread_rows(cell, given, row, count):
    size = cell.shape[1]
    here = jnp.where(iota((BK, size), 0) == cell % BK, 1.0, 0.0).astype(BF16)
    hit = iota((count, size), 0) == row
    picks = [jnp.where(hit, part.astype(F32), 0.0).astype(BF16) for part in three(given)]
    out = lax.dot_general(
        jnp.concatenate(picks, axis=0), here, (((1,), (1,)), ((), ())), preferred_element_type=F32
    )
    return out[:count] + out[count : 2 * count] + out[2 * count :]


def middle_kernel(*refs):
    (from_low, from_high, own_list, sums, info) = refs[5:10]
    block, (up, down, load) = refs[10:15], refs[15:18]
    for f in range(5):
        flat, m = lines(block[f]), COLS[f]
        for c in range(m):
            at = (COL_AT[f] + c) * BI
            flat[pl.ds(4 * EC + LO + 4 - m + c, BI, stride=EC), :] = from_low[at : at + BI, :]
            flat[pl.ds(4 * EC + HI + c, BI, stride=EC), :] = from_high[at : at + BI, :]
    total = jnp.sum(sums[...], axis=0, keepdims=True)
    filled = pltpu.roll(jnp.broadcast_to(total, (8, BK)), BK - 32, 1)[:1]
    value = thrust * (target_speed - total / jnp.maximum(filled, 1.0))
    value = jnp.broadcast_to(jnp.where(iota((1, BK), 1) < 32, value, 0.0), (8, BK))
    load[...] = value

    cell, owner, share = listed(own_list, from_low, from_high)
    i, j = cell // (BJ * BK), (cell // BK) % BJ
    side = iota(cell.shape, 1) // DMAX
    edge = jnp.where(i < 3, i, jnp.where(i >= BI - 3, i - (BI - 6), -1))
    own_row = jnp.where(edge >= 0, edge * BJ + j, -1)
    corner = jnp.where(i < 2, i, jnp.where(i >= BI - 2, i - (BI - 4), -1))
    first = jnp.where(side == 1, BJ - 2, 0)
    across = j - first
    near = (corner >= 0) & (across >= 0) & (across < 2)
    side_row = jnp.where(near, 6 * BJ + (side - 1) * 8 + corner * 2 + across, -1)
    row = jnp.where(side == 0, own_row, side_row)
    force = spread_rows(cell, list_load(owner, share, value), row, 6 * BJ + 16)

    for f in range(5):
        n = LAYERS[f]
        for q in range(n):
            at = (LAYER_AT[f] + q) * WIDE
            for ref, l in ((up, 4 + BI - n + q), (down, 4 + q)):
                ref[at : at + BJ, :] = block[f][l, OWN : OWN + BJ, :]
                ref[at + BJ : at + BJ + 4, :] = block[f][l, LO : LO + 4, :]
                ref[at + BJ + 4 : at + WIDE, :] = block[f][l, HI : HI + 4, :]
    for q in range(3):
        at = (FORCE_AT + q) * WIDE
        for ref, e, c in ((up, 3 + q, 1 + q), (down, q, q)):
            ref[at : at + BJ, :] = force[e * BJ : (e + 1) * BJ]
            ref[at + BJ : at + WIDE, :] = jnp.zeros((8, BK), F32)
            if (ref is up and q > 0) or (ref is down and q < 2):
                low = 6 * BJ + 2 * c
                ref[at + BJ + 2 : at + BJ + 4, :] = force[low : low + 2]
                ref[at + BJ + 4 : at + BJ + 6, :] = force[low + 8 : low + 10]
    for ref in (up, down):
        ref[S_FACE : S_FACE + 8, :] = info[...]


def images(ref, start, count, low_turned, high_turned, outer=True):
    flat = lines(ref)
    backward = BK - 1 - iota((count, BK), 1)
    for source, target, mask in (
        (LO + 3, LO_IN, low_turned),
        (HI, HI_IN, high_turned),
        (OWN, LO_OUT, low_turned),
        (OWN + BJ - 1, HI_OUT, high_turned),
    )[: 4 if outer else 2]:
        value = flat[pl.ds(start * EC + source, count, stride=EC), :]
        mirror = jnp.take_along_axis(value, backward, axis=1, mode="promise_in_bounds")
        flat[pl.ds(start * EC + target, count, stride=EC), :] = jnp.where(mask, mirror, value)


MID, LEFT, RIGHT = slice(8, 40), slice(7, 39), slice(9, 41)
NEAR, NEAR_LEFT, NEAR_RIGHT = slice(OWN, OWN + BJ), slice(OWN - 1, OWN + BJ - 1), slice(OWN + 1, OWN + BJ + 1)


def below(x, sign):
    return jnp.where(iota(x.shape, 1) == 0, sign * x, pltpu.roll(x, 1, 1))


def above(x):
    return jnp.where(iota(x.shape, 1) == BK - 1, 0.0, pltpu.roll(x, BK - 1, 1))


def star_layer(block, force, star, l):
    e = block[4][l, MID, :]
    share = 1.0 / (1.0 + 3.0 * e)
    half = 0.5 * e
    p = block[3]
    q = p[l, MID, :]
    slope = (
        p[l + 1, MID, :] - p[l - 1, MID, :],
        p[l, RIGHT, :] - p[l, LEFT, :],
        above(q) - below(q, 1.0),
    )
    for c in range(3):
        u = block[c]
        x, a, b = u[l, MID, :], u[l - 1, MID, :], u[l + 1, MID, :]
        around = a + b + u[l, LEFT, :] + u[l, RIGHT, :] + below(x, -1.0) + above(x)
        value = x - 0.125 * (b - a) + half * around - 0.25 * slope[c]
        if c == 0:
            value = value + 0.5 * force[l, MID, :]
        star[c][l, MID, :] = value * share


def sweep_layer(star, sweep, l):
    x = star[2][l, MID, :]
    total = (star[0][l + 1, MID, :] - star[0][l - 1, MID, :]) + (star[1][l, RIGHT, :] - star[1][l, LEFT, :])
    sweep[l, MID, :] = (total + (above(x) - below(x, -1.0))) * (-1.0 / 6.0)


def second_layer(sweep, second, l):
    x = sweep[l, MID, :]
    around = sweep[l - 1, MID, :] + sweep[l + 1, MID, :] + sweep[l, LEFT, :] + sweep[l, RIGHT, :]
    second[l, MID, :] = (around + below(x, 1.0) + above(x)) * (1.0 / 6.0) + x


def out_layer(block, star, second, stage, l, at):
    x = second[l, NEAR, :]
    slope = (
        second[l + 1, NEAR, :] - second[l - 1, NEAR, :],
        second[l, NEAR_RIGHT, :] - second[l, NEAR_LEFT, :],
        above(x) - below(x, 1.0),
    )
    for c in range(3):
        stage[c, at] = star[c][l, NEAR, :] - 0.25 * slope[c]
    stage[3, at] = block[3][l, NEAR, :] + x


def layers(start, stop, step, unroll):
    def run(l, carry):
        step(l)
        return carry

    lax.fori_loop(start, stop, run, 0, unroll=unroll)


def inner_kernel(*refs):
    from_low, from_high, own_list, load, info = refs[5:10]
    block, star, (force, sweep, second) = refs[10:15], refs[15:18], refs[18:21]
    stage = refs[21]
    cell, owner, share = listed(own_list, from_low, from_high)
    given = list_load(owner, share, load[...])
    i, j = cell // (BJ * BK), (cell // BK) % BJ
    own, low, high = (slice(n * DMAX, (n + 1) * DMAX) for n in range(3))
    out = spread_rows(cell[:, own], given[:, own], cell[:, own] // BK, CELLS)
    force[4 : 4 + BI, NEAR, :] = out.reshape(BI, BJ, BK)
    flat = lines(force)
    for part, j0, at in ((low, BJ - 2, LO + 2), (high, 0, HI)):
        across = j[:, part] - j0
        row = jnp.where((across >= 0) & (across < 2), across * BI + i[:, part], -1)
        out = spread_rows(cell[:, part], given[:, part], row, 2 * BI)
        for c in range(2):
            flat[pl.ds(4 * EC + at + c, BI, stride=EC), :] = out[c * BI : (c + 1) * BI]
    low_turned, high_turned = info[0:1, :] > 0.5, info[1:2, :] > 0.5
    a, b = INNER
    for f in range(4):
        images(block[f], 4, BI, low_turned, high_turned)
    layers(a - 3, b + 3, lambda l: star_layer(block, force, star, l), 2)
    images(star[1], a - 3, b - a + 6, low_turned, high_turned)
    layers(a - 2, b + 2, lambda l: sweep_layer(star, sweep, l), 4)
    images(sweep, a - 2, b - a + 4, low_turned, high_turned)
    layers(a - 1, b + 1, lambda l: second_layer(sweep, second, l), 2)
    images(second, a - 1, b - a + 2, low_turned, high_turned, outer=False)
    layers(a, b, lambda l: out_layer(block, star, second, stage, l, l - a), 4)


def outer_kernel(*refs):
    from_up, from_down, info, done = refs[11:15]
    refs = refs[15:]
    block, star, (force, sweep, second) = refs[:5], refs[5:8], refs[8:11]
    vel_out, prs_out, stage, sem = refs[11:]
    a, b = INNER
    inside = slice(a - 4, b - 4)
    copies = [pltpu.make_async_copy(done.at[c], vel_out.at[c, inside], sem.at[8 + c]) for c in range(3)]
    copies.append(pltpu.make_async_copy(done.at[3], prs_out.at[inside], sem.at[11]))
    for copy in copies:
        copy.start()
    place = lax.axis_index("stream")
    first_row = place == 0
    last_row = place == lax.axis_size("stream") - 1
    for f in range(6):
        to, n, base = (block[f], LAYERS[f], LAYER_AT[f]) if f < 5 else (force, 3, FORCE_AT)
        for q in range(n):
            at = (base + q) * WIDE
            for ref, l in ((from_up, 4 - n + q), (from_down, 4 + BI + q)):
                to[l, OWN : OWN + BJ, :] = ref[at : at + BJ, :]
                to[l, LO : LO + 4, :] = ref[at + BJ : at + BJ + 4, :]
                to[l, HI : HI + 4, :] = ref[at + BJ + 4 : at + WIDE, :]

    def both(ref, down, outer=True):
        for start, other in ((down, from_up), (EL - 4 - down, from_down)):
            l = iota((4, BK), 0) + start
            here = (l >= 4) & (l < 4 + BI)
            low = jnp.where(here, info[0:1, :], other[S_FACE : S_FACE + 1, :]) > 0.5
            high = jnp.where(here, info[1:2, :], other[S_FACE + 1 : S_FACE + 2, :]) > 0.5
            images(ref, start, 4, low, high, outer)

    def ends(down, step):
        for l in (*range(down, down + 4), *range(EL - 4 - down, EL - down)):
            step(l)

    @pl.when(first_row)
    def _():
        for f in range(3):
            block[f][3] = jnp.zeros((EC, BK), F32)
        block[3][3] = block[3][4]

    @pl.when(last_row)
    def _():
        for f in range(3):
            block[f][4 + BI] = block[f][3 + BI]
        block[3][4 + BI] = jnp.zeros((EC, BK), F32)

    for f in range(4):
        both(block[f], 0)
    ends(1, lambda l: star_layer(block, force, star, l))

    @pl.when(first_row)
    def _():
        star[0][3] = jnp.zeros((EC, BK), F32)

    @pl.when(last_row)
    def _():
        star[0][4 + BI] = star[0][3 + BI]

    both(star[1], 1)
    ends(2, lambda l: sweep_layer(star, sweep, l))

    @pl.when(first_row)
    def _():
        sweep[3] = sweep[4]

    @pl.when(last_row)
    def _():
        sweep[4 + BI] = jnp.zeros((EC, BK), F32)

    both(sweep, 2)
    ends(3, lambda l: second_layer(sweep, second, l))

    @pl.when(first_row)
    def _():
        second[3] = second[4]

    @pl.when(last_row)
    def _():
        second[4 + BI] = jnp.zeros((EC, BK), F32)

    both(second, 3, outer=False)
    both(second, 4, outer=False)
    for start in (4, b):
        at = 0 if start == 4 else 4
        for q in range(4):
            out_layer(block, star, second, stage, start + q, at + q)
        part, to = slice(at, at + 4), slice(start - 4, start)
        for c in range(3):
            copies.append(pltpu.make_async_copy(stage.at[c, part], vel_out.at[c, to], sem.at[at + c]))
        copies.append(pltpu.make_async_copy(stage.at[3, part], prs_out.at[to], sem.at[at + 3]))
        for copy in copies[at + 4 :]:
            copy.start()
    for copy in copies:
        copy.wait()


def body(velocity, pressure, turb_k, turb_omega, face_code, disc_cells, disc_sector, disc_weight):
    streams, girths = lax.axis_size("stream"), lax.axis_size("girth")
    vmem = pl.BlockSpec(memory_space=pltpu.VMEM)
    hbm = pl.BlockSpec(memory_space=pltpu.HBM)
    params = pltpu.CompilerParams(vmem_limit_bytes=24 * 2**20)

    def struct(*shape):
        return jax.ShapeDtypeStruct(shape, F32)

    block = struct(EL, EC, BK)
    fields = (velocity, pressure, turb_k, turb_omega, disc_cells, disc_sector.reshape(1, DMAX), disc_weight, face_code)
    *exts, sums, to_high, to_low, info = pl.pallas_call(
        head_kernel,
        out_shape=(block,) * 5 + (struct(girths, BK), struct(G_ROWS, BK), struct(G_ROWS, BK), struct(8, BK)),
        in_specs=[hbm] * 8,
        out_specs=(vmem,) * 9,
        scratch_shapes=[
            pltpu.VMEM((BI, BJ, BK), F32),
            pltpu.VMEM((BI, BJ, BK), F32),
            pltpu.VMEM((1, DMAX), I32),
            pltpu.VMEM((1, DMAX), I32),
            pltpu.VMEM((1, DMAX), F32),
            pltpu.SMEM((1, 1, 2), I32),
            pltpu.SemaphoreType.DMA((10,)),
        ],
        compiler_params=params,
        name="head",
    )(*(pltpu.with_memory_space_constraint(x, pltpu.HBM) for x in fields))
    ring = [(g, (g + 1) % girths) for g in range(girths)]
    from_low = lax.ppermute(to_high, "girth", ring)
    from_high = lax.ppermute(to_low, "girth", [(b, a) for a, b in ring])
    sums = lax.all_to_all(sums, "girth", split_axis=0, concat_axis=0, tiled=True)

    *exts, up, down, load = pl.pallas_call(
        middle_kernel,
        out_shape=(block,) * 5 + (struct(S_ROWS, BK), struct(S_ROWS, BK), struct(8, BK)),
        in_specs=[vmem] * 10,
        out_specs=(vmem,) * 8,
        input_output_aliases={n: n for n in range(5)},
        compiler_params=params,
        name="middle",
    )(*exts, from_low, from_high, to_low, sums, info)
    chain = [(s, s + 1) for s in range(streams - 1)]
    from_up = lax.ppermute(up, "stream", chain)
    from_down = lax.ppermute(down, "stream", [(b, a) for a, b in chain])

    outs = (struct(3, BI, BJ, BK), struct(BI, BJ, BK))
    *exts, done = pl.pallas_call(
        inner_kernel,
        out_shape=(block,) * 11 + (struct(4, INNER[1] - INNER[0], BJ, BK),),
        in_specs=[vmem] * 10,
        out_specs=(vmem,) * 12,
        input_output_aliases={n: n for n in range(5)},
        compiler_params=params,
        name="inner",
    )(*exts, from_low, from_high, to_low, load, info)
    return tuple(
        pl.pallas_call(
            outer_kernel,
            out_shape=(block,) * 11 + outs,
            in_specs=[vmem] * 15,
            out_specs=(vmem,) * 11 + (hbm,) * 2,
            input_output_aliases={n: n for n in range(11)},
            scratch_shapes=[pltpu.VMEM((4, 8, BJ, BK), F32), pltpu.SemaphoreType.DMA((12,))],
            compiler_params=params,
            name="outer",
        )(*exts, from_up, from_down, info, done)[11:]
    )


def solution(mesh):
    block = P("stream", "girth", None)
    placed = (P(None, "stream", "girth", None), block, block, block, block, P("stream", "girth"), block, P("stream", "girth"))
    return jax.shard_map(
        body,
        mesh=mesh,
        in_specs=placed,
        out_specs=(P(None, "stream", "girth", None), block),
        check_vma=False,
    )
```

```python
import jax
import jax.numpy as jnp
from jax import lax
from jax.experimental import pallas as pl
from jax.experimental.pallas import tpu as pltpu
from jax.sharding import PartitionSpec as P

viscosity = 0.02
thrust = 8.0
target_speed = 0.5

BI, BJ, BK, DMAX = 32, 16, 128, 512
CELLS = BI * BJ
COLS = (3, 4, 3, 4, 3)
COL_AT = (0, 3, 7, 10, 14)
LAYERS = (4, 3, 3, 4, 3)
LAYER_AT = (0, 4, 7, 10, 14)
LIST_ROWS = 12
G_LIST = 17 * BI
G_ROWS = G_LIST + 16
WIDE = BJ + 8
FORCE_AT = 17
S_FACE = 20 * WIDE
S_ROWS = S_FACE + 8
INNER = (8, 32)
EL, EC = BI + 8, 48
LO, LO_OUT, LO_IN, OWN, HI_IN, HI_OUT, HI = 10, 14, 15, 16, 32, 33, 34
F32, BF16, I32 = jnp.float32, jnp.bfloat16, jnp.int32


def iota(shape, dim):
    return lax.broadcasted_iota(I32, shape, dim)


def is_odd(axis):
    return lax.axis_index(axis) % 2 == 1


def by_parity(axis, even, odd):
    flag = is_odd(axis)
    pl.when(jnp.logical_not(flag))(even)
    pl.when(flag)(odd)


def three(x):
    a = x.astype(BF16)
    rest = x - a.astype(F32)
    b = rest.astype(BF16)
    c = (rest - b.astype(F32)).astype(BF16)
    return a, b, c


def wide_row(ref, at):
    return jnp.concatenate([ref[at + q : at + q + 1, :] for q in range(4)], axis=1)


def lines(ref):
    return ref.reshape(EL * EC, BK)


def put_row(ref, at, row):
    for q in range(4):
        ref[at + q : at + q + 1, :] = row[:, q * BK : (q + 1) * BK]


def head_kernel(vel, prs, tk, tw, cells, sector, weight, face, *refs):
    block, (sums, pack_a, pack_b, info) = refs[:5], refs[5:9]
    k_buf, w_buf, cell_buf, owner_buf, share_buf, face_buf, sem = refs[9:]
    inside = (slice(4, 4 + BI), slice(OWN, OWN + BJ))
    pairs = (
        (cells, cell_buf),
        (sector, owner_buf),
        (weight, share_buf),
        (face, face_buf),
        (vel.at[0], block[0].at[inside]),
        (vel.at[1], block[1].at[inside]),
        (vel.at[2], block[2].at[inside]),
        (prs, block[3].at[inside]),
        (tk, k_buf),
        (tw, w_buf),
    )
    copies = [pltpu.make_async_copy(a, b, sem.at[n]) for n, (a, b) in enumerate(pairs)]
    for copy in copies:
        copy.start()
    for copy in copies[:4]:
        copy.wait()
    cell, owner, share = cell_buf[...], owner_buf[...], share_buf[...]
    for ref in (pack_a, pack_b):
        put_row(ref, G_LIST, cell.astype(F32))
        put_row(ref, G_LIST + 4, owner.astype(F32))
        put_row(ref, G_LIST + 8, share)
        ref[G_LIST + LIST_ROWS : G_ROWS, :] = jnp.zeros((4, BK), F32)
    row = iota((8, BK), 0)
    sides = jnp.where(row == 0, face_buf[0, 0, 0], jnp.where(row == 1, face_buf[0, 0, 1], 0))
    info[...] = sides.astype(F32)
    pick = jnp.where(iota((CELLS, DMAX), 0) == cell // BK, 1.0, 0.0).astype(BF16)
    mine = iota((64, DMAX), 0)
    copies[4].wait()
    parts = jnp.concatenate(three(block[0][inside].reshape(CELLS, BK)), axis=1)
    found = lax.dot_general(parts, pick, (((0,), (0,)), ((), ())), preferred_element_type=F32)
    found = found[:BK] + found[BK : 2 * BK] + found[2 * BK :]
    inflow = jnp.sum(jnp.where(iota((BK, DMAX), 0) == cell % BK, found, 0.0), axis=0, keepdims=True)
    both = jnp.where(mine == owner, inflow, 0.0) + jnp.where(mine == owner + 32, 1.0, 0.0)
    both = jnp.concatenate([both, jnp.zeros((64, DMAX), F32)], axis=0)
    total = lax.dot_general(
        jnp.ones((8, DMAX), F32),
        both,
        (((1,), (1,)), ((), ())),
        precision=lax.Precision.HIGHEST,
        preferred_element_type=F32,
    )
    for t in range(sums.shape[0] // 8):
        sums[t * 8 : t * 8 + 8, :] = total
    for n in (5, 6, 7, 8, 9):
        copies[n].wait()
    block[4][inside] = viscosity + k_buf[...] / w_buf[...]

    def pack(to_high, to_low):
        for f in range(5):
            flat, n = lines(block[f]), COLS[f]
            for c in range(n):
                at = (COL_AT[f] + c) * BI
                to_high[at : at + BI, :] = flat[pl.ds(4 * EC + OWN + BJ - n + c, BI, stride=EC), :]
                to_low[at : at + BI, :] = flat[pl.ds(4 * EC + OWN + c, BI, stride=EC), :]

    by_parity("girth", lambda: pack(pack_a, pack_b), lambda: pack(pack_b, pack_a))


def listed(own, pair_a, pair_b):
    flag = is_odd("girth")
    rows = []
    for at in (G_LIST, G_LIST + 4, G_LIST + 8):
        a, b = wide_row(pair_a, at), wide_row(pair_b, at)
        rows.append(jnp.concatenate([wide_row(own, at), jnp.where(flag, a, b), jnp.where(flag, b, a)], axis=1))
    return rows[0].astype(I32), rows[1].astype(I32), rows[2]


def list_load(owner, share, load):
    mine = jnp.where(iota((32, owner.shape[1]), 0) == owner, 1.0, 0.0)
    given = jnp.dot(load[:, :32], mine, precision=lax.Precision.HIGHEST, preferred_element_type=F32)
    return given[:1] * share


def spread_rows(cell, given, row, count):
    size = cell.shape[1]
    here = jnp.where(iota((BK, size), 0) == cell % BK, 1.0, 0.0).astype(BF16)
    hit = iota((count, size), 0) == row
    picks = [jnp.where(hit, part.astype(F32), 0.0).astype(BF16) for part in three(given)]
    out = lax.dot_general(
        jnp.concatenate(picks, axis=0), here, (((1,), (1,)), ((), ())), preferred_element_type=F32
    )
    return out[:count] + out[count : 2 * count] + out[2 * count :]


def middle_kernel(*refs):
    (pair_a, pair_b, own_list, sums, info) = refs[5:10]
    block, (pack_b, pack_a, spots), (force,) = refs[10:15], refs[15:18], refs[18:]

    def fill(from_low, from_high):
        for f in range(5):
            flat, m = lines(block[f]), COLS[f]
            for c in range(m):
                at = (COL_AT[f] + c) * BI
                flat[pl.ds(4 * EC + LO + 4 - m + c, BI, stride=EC), :] = from_low[at : at + BI, :]
                flat[pl.ds(4 * EC + HI + c, BI, stride=EC), :] = from_high[at : at + BI, :]

    by_parity("girth", lambda: fill(pair_b, pair_a), lambda: fill(pair_a, pair_b))
    total = jnp.sum(sums[...], axis=0, keepdims=True)
    filled = pltpu.roll(jnp.broadcast_to(total, (8, BK)), BK - 32, 1)[:1]
    value = thrust * (target_speed - total / jnp.maximum(filled, 1.0))
    value = jnp.broadcast_to(jnp.where(iota((1, BK), 1) < 32, value, 0.0), (8, BK))
    cell, owner, share = listed(own_list, pair_a, pair_b)
    given = list_load(owner, share, value)
    spots[0:1, :] = cell.astype(F32)
    spots[1:2, :] = given
    i, j = cell // (BJ * BK), (cell // BK) % BJ
    side = iota(cell.shape, 1) // DMAX
    edge = jnp.where(i < 3, i, jnp.where(i >= BI - 3, i - (BI - 6), -1))
    own_row = jnp.where(edge >= 0, edge * BJ + j, -1)
    corner = jnp.where(i < 2, i, jnp.where(i >= BI - 2, i - (BI - 4), -1))
    first = jnp.where(side == 1, BJ - 2, 0)
    across = j - first
    near = (corner >= 0) & (across >= 0) & (across < 2)
    side_row = jnp.where(near, 6 * BJ + (side - 1) * 8 + corner * 2 + across, -1)
    row = jnp.where(side == 0, own_row, side_row)
    force[...] = spread_rows(cell, given, row, 6 * BJ + 16)
    by_parity(
        "stream",
        lambda: stream_packs(block, force, info, pack_a, pack_b),
        lambda: stream_packs(block, force, info, pack_b, pack_a),
    )


def stream_packs(block, force, info, up, down):
    for f in range(5):
        n = LAYERS[f]
        for q in range(n):
            at = (LAYER_AT[f] + q) * WIDE
            for ref, l in ((up, 4 + BI - n + q), (down, 4 + q)):
                ref[at : at + BJ, :] = block[f][l, OWN : OWN + BJ, :]
                ref[at + BJ : at + BJ + 4, :] = block[f][l, LO : LO + 4, :]
                ref[at + BJ + 4 : at + WIDE, :] = block[f][l, HI : HI + 4, :]
    for q in range(3):
        at = (FORCE_AT + q) * WIDE
        for ref, e, c in ((up, 3 + q, 1 + q), (down, q, q)):
            ref[at : at + BJ, :] = force[e * BJ : (e + 1) * BJ]
            ref[at + BJ : at + WIDE, :] = jnp.zeros((8, BK), F32)
            if (ref is up and q > 0) or (ref is down and q < 2):
                low = 6 * BJ + 2 * c
                ref[at + BJ + 2 : at + BJ + 4, :] = force[low : low + 2]
                ref[at + BJ + 4 : at + BJ + 6, :] = force[low + 8 : low + 10]
    for ref in (up, down):
        ref[S_FACE : S_FACE + 8, :] = info[...]


def images(ref, start, count, low_turned, high_turned, outer=True):
    flat = lines(ref)
    backward = BK - 1 - iota((count, BK), 1)
    for source, target, mask in (
        (LO + 3, LO_IN, low_turned),
        (HI, HI_IN, high_turned),
        (OWN, LO_OUT, low_turned),
        (OWN + BJ - 1, HI_OUT, high_turned),
    )[: 4 if outer else 2]:
        value = flat[pl.ds(start * EC + source, count, stride=EC), :]
        mirror = jnp.take_along_axis(value, backward, axis=1, mode="promise_in_bounds")
        flat[pl.ds(start * EC + target, count, stride=EC), :] = jnp.where(mask, mirror, value)


MID, LEFT, RIGHT = slice(8, 40), slice(7, 39), slice(9, 41)
NEAR, NEAR_LEFT, NEAR_RIGHT = slice(OWN, OWN + BJ), slice(OWN - 1, OWN + BJ - 1), slice(OWN + 1, OWN + BJ + 1)


def below(x, sign):
    return jnp.where(iota(x.shape, 1) == 0, sign * x, pltpu.roll(x, 1, 1))


def above(x):
    return jnp.where(iota(x.shape, 1) == BK - 1, 0.0, pltpu.roll(x, BK - 1, 1))


def star_layer(block, force, star, l):
    e = block[4][l, MID, :]
    share = 1.0 / (1.0 + 3.0 * e)
    half = 0.5 * e
    p = block[3]
    q = p[l, MID, :]
    slope = (
        p[l + 1, MID, :] - p[l - 1, MID, :],
        p[l, RIGHT, :] - p[l, LEFT, :],
        above(q) - below(q, 1.0),
    )
    for c in range(3):
        u = block[c]
        x, a, b = u[l, MID, :], u[l - 1, MID, :], u[l + 1, MID, :]
        around = a + b + u[l, LEFT, :] + u[l, RIGHT, :] + below(x, -1.0) + above(x)
        value = x - 0.125 * (b - a) + half * around - 0.25 * slope[c]
        if c == 0:
            value = value + 0.5 * force[l, MID, :]
        star[c][l, MID, :] = value * share


def sweep_layer(star, sweep, l):
    x = star[2][l, MID, :]
    total = (star[0][l + 1, MID, :] - star[0][l - 1, MID, :]) + (star[1][l, RIGHT, :] - star[1][l, LEFT, :])
    sweep[l, MID, :] = (total + (above(x) - below(x, -1.0))) * (-1.0 / 6.0)


def second_layer(sweep, second, l):
    x = sweep[l, MID, :]
    around = sweep[l - 1, MID, :] + sweep[l + 1, MID, :] + sweep[l, LEFT, :] + sweep[l, RIGHT, :]
    second[l, MID, :] = (around + below(x, 1.0) + above(x)) * (1.0 / 6.0) + x


def out_layer(block, star, second, stage, l, at):
    x = second[l, NEAR, :]
    slope = (
        second[l + 1, NEAR, :] - second[l - 1, NEAR, :],
        second[l, NEAR_RIGHT, :] - second[l, NEAR_LEFT, :],
        above(x) - below(x, 1.0),
    )
    for c in range(3):
        stage[c, at] = star[c][l, NEAR, :] - 0.25 * slope[c]
    stage[3, at] = block[3][l, NEAR, :] + x


def layers(start, stop, step, unroll):
    def run(l, carry):
        step(l)
        return carry

    lax.fori_loop(start, stop, run, 0, unroll=unroll)


def inner_kernel(*refs):
    spots, info = refs[5], refs[6].at[S_FACE : S_FACE + 8, :]
    block, star, (force, sweep, second) = refs[7:12], refs[12:15], refs[15:18]
    stage = refs[18]
    cell, given = spots[0:1, :].astype(I32), spots[1:2, :]
    i, j = cell // (BJ * BK), (cell // BK) % BJ
    own, low, high = (slice(n * DMAX, (n + 1) * DMAX) for n in range(3))
    out = spread_rows(cell[:, own], given[:, own], cell[:, own] // BK, CELLS)
    force[4 : 4 + BI, NEAR, :] = out.reshape(BI, BJ, BK)
    flat = lines(force)
    for part, j0, at in ((low, BJ - 2, LO + 2), (high, 0, HI)):
        across = j[:, part] - j0
        row = jnp.where((across >= 0) & (across < 2), across * BI + i[:, part], -1)
        out = spread_rows(cell[:, part], given[:, part], row, 2 * BI)
        for c in range(2):
            flat[pl.ds(4 * EC + at + c, BI, stride=EC), :] = out[c * BI : (c + 1) * BI]
    low_turned, high_turned = info[0:1, :] > 0.5, info[1:2, :] > 0.5
    a, b = INNER
    for f in range(4):
        images(block[f], 4, BI, low_turned, high_turned)
    layers(a - 3, b + 3, lambda l: star_layer(block, force, star, l), 15)
    images(star[1], a - 3, b - a + 6, low_turned, high_turned)
    layers(a - 2, b + 2, lambda l: sweep_layer(star, sweep, l), 28)
    images(sweep, a - 2, b - a + 4, low_turned, high_turned)
    layers(a - 1, b + 1, lambda l: second_layer(sweep, second, l), 26)
    images(second, a - 1, b - a + 2, low_turned, high_turned, outer=False)
    layers(a, b, lambda l: out_layer(block, star, second, stage, l, l - a), 8)


def outer_kernel(*refs):
    pair_a, pair_b, info, done = refs[11:15]
    refs = refs[15:]
    block, star, (force, sweep, second) = refs[:5], refs[5:8], refs[8:11]
    vel_out, prs_out, stage, sem = refs[11:]
    a, b = INNER
    inside = slice(a - 4, b - 4)
    copies = [pltpu.make_async_copy(done.at[c], vel_out.at[c, inside], sem.at[8 + c]) for c in range(3)]
    copies.append(pltpu.make_async_copy(done.at[3], prs_out.at[inside], sem.at[11]))
    for copy in copies:
        copy.start()
    place = lax.axis_index("stream")
    first_row = place == 0
    last_row = place == lax.axis_size("stream") - 1

    def fill(from_up, from_down):
        for f in range(6):
            to, n, base = (block[f], LAYERS[f], LAYER_AT[f]) if f < 5 else (force, 3, FORCE_AT)
            for q in range(n):
                at = (base + q) * WIDE
                for ref, l in ((from_up, 4 - n + q), (from_down, 4 + BI + q)):
                    to[l, OWN : OWN + BJ, :] = ref[at : at + BJ, :]
                    to[l, LO : LO + 4, :] = ref[at + BJ : at + BJ + 4, :]
                    to[l, HI : HI + 4, :] = ref[at + BJ + 4 : at + WIDE, :]

    by_parity("stream", lambda: fill(pair_b, pair_a), lambda: fill(pair_a, pair_b))
    face_a, face_b = pair_a[S_FACE : S_FACE + 8, :], pair_b[S_FACE : S_FACE + 8, :]
    flag = is_odd("stream")
    up_face, down_face = jnp.where(flag, face_a, face_b), jnp.where(flag, face_b, face_a)

    def both(ref, down, outer=True):
        for start, other in ((down, up_face), (EL - 4 - down, down_face)):
            l = iota((4, BK), 0) + start
            here = (l >= 4) & (l < 4 + BI)
            low = jnp.where(here, info[0:1, :], other[0:1, :]) > 0.5
            high = jnp.where(here, info[1:2, :], other[1:2, :]) > 0.5
            images(ref, start, 4, low, high, outer)

    def ends(down, step):
        for l in (*range(down, down + 4), *range(EL - 4 - down, EL - down)):
            step(l)

    @pl.when(first_row)
    def _():
        for f in range(3):
            block[f][3] = jnp.zeros((EC, BK), F32)
        block[3][3] = block[3][4]

    @pl.when(last_row)
    def _():
        for f in range(3):
            block[f][4 + BI] = block[f][3 + BI]
        block[3][4 + BI] = jnp.zeros((EC, BK), F32)

    for f in range(4):
        both(block[f], 0)
    ends(1, lambda l: star_layer(block, force, star, l))

    @pl.when(first_row)
    def _():
        star[0][3] = jnp.zeros((EC, BK), F32)

    @pl.when(last_row)
    def _():
        star[0][4 + BI] = star[0][3 + BI]

    both(star[1], 1)
    ends(2, lambda l: sweep_layer(star, sweep, l))

    @pl.when(first_row)
    def _():
        sweep[3] = sweep[4]

    @pl.when(last_row)
    def _():
        sweep[4 + BI] = jnp.zeros((EC, BK), F32)

    both(sweep, 2)
    ends(3, lambda l: second_layer(sweep, second, l))

    @pl.when(first_row)
    def _():
        second[3] = second[4]

    @pl.when(last_row)
    def _():
        second[4 + BI] = jnp.zeros((EC, BK), F32)

    both(second, 3, outer=False)
    both(second, 4, outer=False)
    for start in (4, b):
        at = 0 if start == 4 else 4
        for q in range(4):
            out_layer(block, star, second, stage, start + q, at + q)
        part, to = slice(at, at + 4), slice(start - 4, start)
        for c in range(3):
            copies.append(pltpu.make_async_copy(stage.at[c, part], vel_out.at[c, to], sem.at[at + c]))
        copies.append(pltpu.make_async_copy(stage.at[3, part], prs_out.at[to], sem.at[at + 3]))
        for copy in copies[at + 4 :]:
            copy.start()
    for copy in copies:
        copy.wait()


def body(velocity, pressure, turb_k, turb_omega, face_code, disc_cells, disc_sector, disc_weight):
    streams, girths = lax.axis_size("stream"), lax.axis_size("girth")
    vmem = pl.BlockSpec(memory_space=pltpu.VMEM)
    hbm = pl.BlockSpec(memory_space=pltpu.HBM)
    params = pltpu.CompilerParams(vmem_limit_bytes=24 * 2**20)

    def struct(*shape):
        return jax.ShapeDtypeStruct(shape, F32)

    block = struct(EL, EC, BK)
    fields = (velocity, pressure, turb_k, turb_omega, disc_cells, disc_sector.reshape(1, DMAX), disc_weight, face_code)
    *exts, sums, pack_a, pack_b, info = pl.pallas_call(
        head_kernel,
        out_shape=(block,) * 5 + (struct(girths, BK), struct(G_ROWS, BK), struct(G_ROWS, BK), struct(8, BK)),
        in_specs=[hbm] * 8,
        out_specs=(vmem,) * 9,
        scratch_shapes=[
            pltpu.VMEM((BI, BJ, BK), F32),
            pltpu.VMEM((BI, BJ, BK), F32),
            pltpu.VMEM((1, DMAX), I32),
            pltpu.VMEM((1, DMAX), I32),
            pltpu.VMEM((1, DMAX), F32),
            pltpu.SMEM((1, 1, 2), I32),
            pltpu.SemaphoreType.DMA((10,)),
        ],
        compiler_params=params,
        name="head",
    )(*(pltpu.with_memory_space_constraint(x, pltpu.HBM) for x in fields))

    def pairs(size, first, cyclic):
        ends = [(n, (n + 1) % size) for n in range(first, size, 2) if cyclic or n + 1 < size]
        return [pair for a, b in ends for pair in ((a, b), (b, a))]

    pair_b = lax.ppermute(pack_b, "girth", pairs(girths, 1, True))
    pair_a = lax.ppermute(pack_a, "girth", pairs(girths, 0, True))
    sums = lax.all_to_all(sums, "girth", split_axis=0, concat_axis=0, tiled=True)

    *exts, up_b, up_a, spots = pl.pallas_call(
        middle_kernel,
        out_shape=(block,) * 5 + (struct(S_ROWS, BK), struct(S_ROWS, BK), struct(8, 3 * DMAX)),
        in_specs=[vmem] * 10,
        out_specs=(vmem,) * 8,
        input_output_aliases={n: n for n in range(5)},
        scratch_shapes=[pltpu.VMEM((6 * BJ + 16, BK), F32)],
        compiler_params=params,
        name="middle",
    )(*exts, pair_a, pair_b, pack_a, sums, info)
    stream_a = lax.ppermute(up_a, "stream", pairs(streams, 0, False))
    stream_b = lax.ppermute(up_b, "stream", pairs(streams, 1, False))

    outs = (struct(3, BI, BJ, BK), struct(BI, BJ, BK))
    *exts, done = pl.pallas_call(
        inner_kernel,
        out_shape=(block,) * 11 + (struct(4, INNER[1] - INNER[0], BJ, BK),),
        in_specs=[vmem] * 7,
        out_specs=(vmem,) * 12,
        input_output_aliases={n: n for n in range(5)},
        compiler_params=params,
        name="inner",
    )(*exts, spots, up_a)
    return tuple(
        pl.pallas_call(
            outer_kernel,
            out_shape=(block,) * 11 + outs,
            in_specs=[vmem] * 15,
            out_specs=(vmem,) * 11 + (hbm,) * 2,
            input_output_aliases={n: n for n in range(11)},
            scratch_shapes=[pltpu.VMEM((4, 8, BJ, BK), F32), pltpu.SemaphoreType.DMA((12,))],
            compiler_params=params,
            name="outer",
        )(*exts, stream_a, stream_b, info, done)[11:]
    )


def solution(mesh):
    block = P("stream", "girth", None)
    placed = (P(None, "stream", "girth", None), block, block, block, block, P("stream", "girth"), block, P("stream", "girth"))
    return jax.shard_map(
        body,
        mesh=mesh,
        in_specs=placed,
        out_specs=(P(None, "stream", "girth", None), block),
        check_vma=False,
    )
```

```python
import jax
import jax.numpy as jnp
from jax import lax
from jax.experimental import pallas as pl
from jax.experimental.pallas import tpu as pltpu
from jax.sharding import PartitionSpec as P

viscosity = 0.02
thrust = 8.0
target_speed = 0.5

BI, BJ, BK, DMAX = 32, 16, 128, 512
CELLS = BI * BJ
COLS = (3, 4, 3, 4, 3)
COL_AT = (0, 3, 7, 10, 14)
LAYERS = (4, 3, 3, 4, 3)
LAYER_AT = (0, 4, 7, 10, 14)
LIST_ROWS = 12
G_LIST = 17 * BI
G_ROWS = G_LIST + 16
FORCE_AT = 17
S_SIDE = 20 * BJ
S_FACE = 392
S_ROWS = S_FACE + 8
INNER = (8, 32)
EL, EC = BI + 8, 48
LO, LO_OUT, LO_IN, OWN, HI_IN, HI_OUT, HI = 10, 14, 15, 16, 32, 33, 34
F32, BF16, I32 = jnp.float32, jnp.bfloat16, jnp.int32


def iota(shape, dim):
    return lax.broadcasted_iota(I32, shape, dim)


def is_odd(axis):
    return lax.axis_index(axis) % 2 == 1


def by_parity(axis, even, odd):
    flag = is_odd(axis)
    pl.when(jnp.logical_not(flag))(even)
    pl.when(flag)(odd)


def three(x):
    a = x.astype(BF16)
    rest = x - a.astype(F32)
    b = rest.astype(BF16)
    c = (rest - b.astype(F32)).astype(BF16)
    return a, b, c


def side_rows(f):
    reach = (4, 4, 4, 4, 3, 3)
    depths = LAYERS + (3,)
    at = S_SIDE
    for g in range(f + 1):
        found = []
        for d in range(1, depths[g] + 1):
            width = reach[g] - d
            found.append((d, at, width))
            at += 2 * width
    return found


def wide_row(ref, at):
    return jnp.concatenate([ref[at + q : at + q + 1, :] for q in range(4)], axis=1)


def lines(ref):
    return ref.reshape(EL * EC, BK)


def put_row(ref, at, row):
    for q in range(4):
        ref[at + q : at + q + 1, :] = row[:, q * BK : (q + 1) * BK]


def head_kernel(vel, prs, tk, tw, cells, sector, weight, face, *refs):
    block, (sums, pack_a, pack_b, info) = refs[:5], refs[5:9]
    k_buf, w_buf, cell_buf, owner_buf, share_buf, face_buf, sem = refs[9:]
    inside = (slice(4, 4 + BI), slice(OWN, OWN + BJ))
    pairs = (
        (cells, cell_buf),
        (sector, owner_buf),
        (weight, share_buf),
        (face, face_buf),
        (vel.at[0], block[0].at[inside]),
        (vel.at[1], block[1].at[inside]),
        (vel.at[2], block[2].at[inside]),
        (prs, block[3].at[inside]),
        (tk, k_buf),
        (tw, w_buf),
    )
    copies = [pltpu.make_async_copy(a, b, sem.at[n]) for n, (a, b) in enumerate(pairs)]
    for copy in copies:
        copy.start()
    for copy in copies[:4]:
        copy.wait()
    cell, owner, share = cell_buf[...], owner_buf[...], share_buf[...]
    for ref in (pack_a, pack_b):
        put_row(ref, G_LIST, cell.astype(F32))
        put_row(ref, G_LIST + 4, owner.astype(F32))
        put_row(ref, G_LIST + 8, share)
        ref[G_LIST + LIST_ROWS : G_ROWS, :] = jnp.zeros((4, BK), F32)
    row = iota((8, BK), 0)
    sides = jnp.where(row == 0, face_buf[0, 0, 0], jnp.where(row == 1, face_buf[0, 0, 1], 0))
    info[...] = sides.astype(F32)
    pick = jnp.where(iota((CELLS, DMAX), 0) == cell // BK, 1.0, 0.0).astype(BF16)
    mine = iota((64, DMAX), 0)
    copies[4].wait()
    parts = jnp.concatenate(three(block[0][inside].reshape(CELLS, BK)), axis=1)
    found = lax.dot_general(parts, pick, (((0,), (0,)), ((), ())), preferred_element_type=F32)
    found = found[:BK] + found[BK : 2 * BK] + found[2 * BK :]
    inflow = jnp.sum(jnp.where(iota((BK, DMAX), 0) == cell % BK, found, 0.0), axis=0, keepdims=True)
    both = jnp.where(mine == owner, inflow, 0.0) + jnp.where(mine == owner + 32, 1.0, 0.0)
    both = jnp.concatenate([both, jnp.zeros((64, DMAX), F32)], axis=0)
    total = lax.dot_general(
        jnp.ones((8, DMAX), F32),
        both,
        (((1,), (1,)), ((), ())),
        precision=lax.Precision.HIGHEST,
        preferred_element_type=F32,
    )
    for t in range(sums.shape[0] // 8):
        sums[t * 8 : t * 8 + 8, :] = total
    def pack(to_high, to_low, fields):
        for f in fields:
            flat, n = lines(block[f]), COLS[f]
            for c in range(n):
                at = (COL_AT[f] + c) * BI
                to_high[at : at + BI, :] = flat[pl.ds(4 * EC + OWN + BJ - n + c, BI, stride=EC), :]
                to_low[at : at + BI, :] = flat[pl.ds(4 * EC + OWN + c, BI, stride=EC), :]

    for waited, fields in (((5, 6, 7), range(4)), ((8, 9), (4,))):
        for n in waited:
            copies[n].wait()
        if 4 in fields:
            block[4][inside] = viscosity + k_buf[...] / w_buf[...]
        by_parity("girth", lambda: pack(pack_a, pack_b, fields), lambda: pack(pack_b, pack_a, fields))


def listed(own, pair_a, pair_b):
    flag = is_odd("girth")
    rows = []
    for at in (G_LIST, G_LIST + 4, G_LIST + 8):
        a, b = wide_row(pair_a, at), wide_row(pair_b, at)
        rows.append(jnp.concatenate([wide_row(own, at), jnp.where(flag, a, b), jnp.where(flag, b, a)], axis=1))
    return rows[0].astype(I32), rows[1].astype(I32), rows[2]


def list_load(owner, share, load):
    mine = jnp.where(iota((32, owner.shape[1]), 0) == owner, 1.0, 0.0)
    given = jnp.dot(load[:, :32], mine, precision=lax.Precision.HIGHEST, preferred_element_type=F32)
    return given[:1] * share


def spread_rows(cell, given, row, count):
    size = cell.shape[1]
    here = jnp.where(iota((BK, size), 0) == cell % BK, 1.0, 0.0).astype(BF16)
    hit = iota((count, size), 0) == row
    picks = [jnp.where(hit, part.astype(F32), 0.0).astype(BF16) for part in three(given)]
    out = lax.dot_general(
        jnp.concatenate(picks, axis=0), here, (((1,), (1,)), ((), ())), preferred_element_type=F32
    )
    return out[:count] + out[count : 2 * count] + out[2 * count :]


def middle_kernel(*refs):
    (pair_a, pair_b, own_list, sums, info) = refs[5:10]
    block, (pack_b, pack_a, spots), (force,) = refs[10:15], refs[15:18], refs[18:]

    def fill(from_low, from_high):
        for f in range(5):
            flat, m = lines(block[f]), COLS[f]
            for c in range(m):
                at = (COL_AT[f] + c) * BI
                flat[pl.ds(4 * EC + LO + 4 - m + c, BI, stride=EC), :] = from_low[at : at + BI, :]
                flat[pl.ds(4 * EC + HI + c, BI, stride=EC), :] = from_high[at : at + BI, :]

    by_parity("girth", lambda: fill(pair_b, pair_a), lambda: fill(pair_a, pair_b))
    total = jnp.sum(sums[...], axis=0, keepdims=True)
    filled = pltpu.roll(jnp.broadcast_to(total, (8, BK)), BK - 32, 1)[:1]
    value = thrust * (target_speed - total / jnp.maximum(filled, 1.0))
    value = jnp.broadcast_to(jnp.where(iota((1, BK), 1) < 32, value, 0.0), (8, BK))
    cell, owner, share = listed(own_list, pair_a, pair_b)
    given = list_load(owner, share, value)
    spots[0:1, :] = cell.astype(F32)
    spots[1:2, :] = given
    i, j = cell // (BJ * BK), (cell // BK) % BJ
    side = iota(cell.shape, 1) // DMAX
    edge = jnp.where(i < 3, i, jnp.where(i >= BI - 3, i - (BI - 6), -1))
    own_row = jnp.where(edge >= 0, edge * BJ + j, -1)
    corner = jnp.where(i < 2, i, jnp.where(i >= BI - 2, i - (BI - 4), -1))
    first = jnp.where(side == 1, BJ - 2, 0)
    across = j - first
    near = (corner >= 0) & (across >= 0) & (across < 2)
    side_row = jnp.where(near, 6 * BJ + (side - 1) * 8 + corner * 2 + across, -1)
    row = jnp.where(side == 0, own_row, side_row)
    force[...] = spread_rows(cell, given, row, 6 * BJ + 16)
    by_parity(
        "stream",
        lambda: stream_packs(block, force, info, pack_a, pack_b),
        lambda: stream_packs(block, force, info, pack_b, pack_a),
    )


def stream_packs(block, force, info, up, down):
    for f in range(5):
        n = LAYERS[f]
        for q in range(n):
            at = (LAYER_AT[f] + q) * BJ
            up[at : at + BJ, :] = block[f][4 + BI - n + q, OWN : OWN + BJ, :]
            down[at : at + BJ, :] = block[f][4 + q, OWN : OWN + BJ, :]
        for d, at, width in side_rows(f):
            if width:
                for ref, l in ((up, 4 + BI - d), (down, 3 + d)):
                    ref[at : at + width, :] = block[f][l, LO + 4 - width : LO + 4, :]
                    ref[at + width : at + 2 * width, :] = block[f][l, HI : HI + width, :]
    for q in range(3):
        at = (FORCE_AT + q) * BJ
        up[at : at + BJ, :] = force[(3 + q) * BJ : (4 + q) * BJ, :]
        down[at : at + BJ, :] = force[q * BJ : (q + 1) * BJ, :]
    for d, at, width in side_rows(5):
        if width:
            for ref, c in ((up, 4 - d), (down, d - 1)):
                low = 6 * BJ + 2 * c
                ref[at : at + width, :] = force[low + 2 - width : low + 2, :]
                ref[at + width : at + 2 * width, :] = force[low + 8 : low + 8 + width, :]
    for ref in (up, down):
        ref[S_FACE : S_FACE + 8, :] = info[...]


def images(ref, start, count, low_turned, high_turned, outer=True):
    flat = lines(ref)
    backward = BK - 1 - iota((count, BK), 1)
    for source, target, mask in (
        (LO + 3, LO_IN, low_turned),
        (HI, HI_IN, high_turned),
        (OWN, LO_OUT, low_turned),
        (OWN + BJ - 1, HI_OUT, high_turned),
    )[: 4 if outer else 2]:
        value = flat[pl.ds(start * EC + source, count, stride=EC), :]
        mirror = jnp.take_along_axis(value, backward, axis=1, mode="promise_in_bounds")
        flat[pl.ds(start * EC + target, count, stride=EC), :] = jnp.where(mask, mirror, value)


MID, LEFT, RIGHT = slice(8, 40), slice(7, 39), slice(9, 41)
NEAR, NEAR_LEFT, NEAR_RIGHT = slice(OWN, OWN + BJ), slice(OWN - 1, OWN + BJ - 1), slice(OWN + 1, OWN + BJ + 1)


def below(x, sign):
    return jnp.where(iota(x.shape, 1) == 0, sign * x, pltpu.roll(x, 1, 1))


def above(x):
    return jnp.where(iota(x.shape, 1) == BK - 1, 0.0, pltpu.roll(x, BK - 1, 1))


def star_layer(block, force, star, l):
    e = block[4][l, MID, :]
    share = 1.0 / (1.0 + 3.0 * e)
    half = 0.5 * e
    p = block[3]
    q = p[l, MID, :]
    slope = (
        p[l + 1, MID, :] - p[l - 1, MID, :],
        p[l, RIGHT, :] - p[l, LEFT, :],
        above(q) - below(q, 1.0),
    )
    for c in range(3):
        u = block[c]
        x, a, b = u[l, MID, :], u[l - 1, MID, :], u[l + 1, MID, :]
        around = a + b + u[l, LEFT, :] + u[l, RIGHT, :] + below(x, -1.0) + above(x)
        value = x - 0.125 * (b - a) + half * around - 0.25 * slope[c]
        if c == 0:
            value = value + 0.5 * force[l, MID, :]
        star[c][l, MID, :] = value * share


def sweep_layer(star, sweep, l):
    x = star[2][l, MID, :]
    total = (star[0][l + 1, MID, :] - star[0][l - 1, MID, :]) + (star[1][l, RIGHT, :] - star[1][l, LEFT, :])
    sweep[l, MID, :] = (total + (above(x) - below(x, -1.0))) * (-1.0 / 6.0)


def second_layer(sweep, second, l):
    x = sweep[l, MID, :]
    around = sweep[l - 1, MID, :] + sweep[l + 1, MID, :] + sweep[l, LEFT, :] + sweep[l, RIGHT, :]
    second[l, MID, :] = (around + below(x, 1.0) + above(x)) * (1.0 / 6.0) + x


def out_layer(block, star, second, stage, l, at):
    x = second[l, NEAR, :]
    slope = (
        second[l + 1, NEAR, :] - second[l - 1, NEAR, :],
        second[l, NEAR_RIGHT, :] - second[l, NEAR_LEFT, :],
        above(x) - below(x, 1.0),
    )
    for c in range(3):
        stage[c, at] = star[c][l, NEAR, :] - 0.25 * slope[c]
    stage[3, at] = block[3][l, NEAR, :] + x


def layers(start, stop, step, unroll):
    def run(l, carry):
        step(l)
        return carry

    lax.fori_loop(start, stop, run, 0, unroll=unroll)


def inner_kernel(*refs):
    spots, info = refs[5], refs[6].at[S_FACE : S_FACE + 8, :]
    block, star, (force, sweep, second) = refs[7:12], refs[12:15], refs[15:18]
    stage = refs[18]
    cell, given = spots[0:1, :].astype(I32), spots[1:2, :]
    i, j = cell // (BJ * BK), (cell // BK) % BJ
    own, low, high = (slice(n * DMAX, (n + 1) * DMAX) for n in range(3))
    out = spread_rows(cell[:, own], given[:, own], cell[:, own] // BK, CELLS)
    force[4 : 4 + BI, NEAR, :] = out.reshape(BI, BJ, BK)
    flat = lines(force)
    for part, j0, at in ((low, BJ - 2, LO + 2), (high, 0, HI)):
        across = j[:, part] - j0
        row = jnp.where((across >= 0) & (across < 2), across * BI + i[:, part], -1)
        out = spread_rows(cell[:, part], given[:, part], row, 2 * BI)
        for c in range(2):
            flat[pl.ds(4 * EC + at + c, BI, stride=EC), :] = out[c * BI : (c + 1) * BI]
    low_turned, high_turned = info[0:1, :] > 0.5, info[1:2, :] > 0.5
    a, b = INNER
    for f in range(4):
        images(block[f], 4, BI, low_turned, high_turned)
    layers(a - 3, b + 3, lambda l: star_layer(block, force, star, l), 15)
    images(star[1], a - 3, b - a + 6, low_turned, high_turned)
    layers(a - 2, b + 2, lambda l: sweep_layer(star, sweep, l), 28)
    images(sweep, a - 2, b - a + 4, low_turned, high_turned)
    layers(a - 1, b + 1, lambda l: second_layer(sweep, second, l), 26)
    images(second, a - 1, b - a + 2, low_turned, high_turned, outer=False)
    layers(a, b, lambda l: out_layer(block, star, second, stage, l, l - a), 8)


def outer_kernel(*refs):
    pair_a, pair_b, info, done = refs[11:15]
    refs = refs[15:]
    block, star, (force, sweep, second) = refs[:5], refs[5:8], refs[8:11]
    vel_out, prs_out, stage, sem = refs[11:]
    a, b = INNER
    inside = slice(a - 4, b - 4)
    copies = [pltpu.make_async_copy(done.at[c], vel_out.at[c, inside], sem.at[8 + c]) for c in range(3)]
    copies.append(pltpu.make_async_copy(done.at[3], prs_out.at[inside], sem.at[11]))
    for copy in copies:
        copy.start()
    place = lax.axis_index("stream")
    first_row = place == 0
    last_row = place == lax.axis_size("stream") - 1

    def fill(from_up, from_down):
        for f in range(6):
            to, n, base = (block[f], LAYERS[f], LAYER_AT[f]) if f < 5 else (force, 3, FORCE_AT)
            for q in range(n):
                at = (base + q) * BJ
                to[4 - n + q, OWN : OWN + BJ, :] = from_up[at : at + BJ, :]
                to[4 + BI + q, OWN : OWN + BJ, :] = from_down[at : at + BJ, :]
            for d, at, width in side_rows(f):
                if width:
                    for ref, l in ((from_up, 4 - d), (from_down, 3 + BI + d)):
                        to[l, LO + 4 - width : LO + 4, :] = ref[at : at + width, :]
                        to[l, HI : HI + width, :] = ref[at + width : at + 2 * width, :]

    by_parity("stream", lambda: fill(pair_b, pair_a), lambda: fill(pair_a, pair_b))
    face_a, face_b = pair_a[S_FACE : S_FACE + 8, :], pair_b[S_FACE : S_FACE + 8, :]
    flag = is_odd("stream")
    up_face, down_face = jnp.where(flag, face_a, face_b), jnp.where(flag, face_b, face_a)

    def both(ref, down, outer=True):
        for start, other in ((down, up_face), (EL - 4 - down, down_face)):
            l = iota((4, BK), 0) + start
            here = (l >= 4) & (l < 4 + BI)
            low = jnp.where(here, info[0:1, :], other[0:1, :]) > 0.5
            high = jnp.where(here, info[1:2, :], other[1:2, :]) > 0.5
            images(ref, start, 4, low, high, outer)

    def ends(down, step):
        for l in (*range(down, down + 4), *range(EL - 4 - down, EL - down)):
            step(l)

    def edges(ref, low, high):
        ref[3, MID, :] = jnp.where(first_row, low, ref[3, MID, :])
        ref[4 + BI, MID, :] = jnp.where(last_row, high, ref[4 + BI, MID, :])

    for ref in block[:3]:
        edges(ref, 0.0, ref[3 + BI, MID, :])
    edges(block[3], block[3][4, MID, :], 0.0)
    for f in range(4):
        both(block[f], 0)
    ends(1, lambda l: star_layer(block, force, star, l))

    edges(star[0], 0.0, star[0][3 + BI, MID, :])
    both(star[1], 1)
    ends(2, lambda l: sweep_layer(star, sweep, l))

    edges(sweep, sweep[4, MID, :], 0.0)
    both(sweep, 2)
    ends(3, lambda l: second_layer(sweep, second, l))

    edges(second, second[4, MID, :], 0.0)
    both(second, 4, outer=False)
    for start in (4, b):
        at = 0 if start == 4 else 4
        for q in range(4):
            out_layer(block, star, second, stage, start + q, at + q)
        part, to = slice(at, at + 4), slice(start - 4, start)
        for c in range(3):
            copies.append(pltpu.make_async_copy(stage.at[c, part], vel_out.at[c, to], sem.at[at + c]))
        copies.append(pltpu.make_async_copy(stage.at[3, part], prs_out.at[to], sem.at[at + 3]))
        for copy in copies[at + 4 :]:
            copy.start()
    for copy in copies:
        copy.wait()


def body(velocity, pressure, turb_k, turb_omega, face_code, disc_cells, disc_sector, disc_weight):
    streams, girths = lax.axis_size("stream"), lax.axis_size("girth")
    vmem = pl.BlockSpec(memory_space=pltpu.VMEM)
    hbm = pl.BlockSpec(memory_space=pltpu.HBM)
    params = pltpu.CompilerParams(vmem_limit_bytes=24 * 2**20)

    def struct(*shape):
        return jax.ShapeDtypeStruct(shape, F32)

    block = struct(EL, EC, BK)
    fields = (velocity, pressure, turb_k, turb_omega, disc_cells, disc_sector.reshape(1, DMAX), disc_weight, face_code)
    *exts, sums, pack_a, pack_b, info = pl.pallas_call(
        head_kernel,
        out_shape=(block,) * 5 + (struct(girths, BK), struct(G_ROWS, BK), struct(G_ROWS, BK), struct(8, BK)),
        in_specs=[hbm] * 8,
        out_specs=(vmem,) * 9,
        scratch_shapes=[
            pltpu.VMEM((BI, BJ, BK), F32),
            pltpu.VMEM((BI, BJ, BK), F32),
            pltpu.VMEM((1, DMAX), I32),
            pltpu.VMEM((1, DMAX), I32),
            pltpu.VMEM((1, DMAX), F32),
            pltpu.SMEM((1, 1, 2), I32),
            pltpu.SemaphoreType.DMA((10,)),
        ],
        compiler_params=params,
        name="head",
    )(*(pltpu.with_memory_space_constraint(x, pltpu.HBM) for x in fields))

    def pairs(size, first, cyclic):
        ends = [(n, (n + 1) % size) for n in range(first, size, 2) if cyclic or n + 1 < size]
        return [pair for a, b in ends for pair in ((a, b), (b, a))]

    pair_b = lax.ppermute(pack_b, "girth", pairs(girths, 1, True))
    pair_a = lax.ppermute(pack_a, "girth", pairs(girths, 0, True))
    sums = lax.all_to_all(sums, "girth", split_axis=0, concat_axis=0, tiled=True)

    *exts, up_b, up_a, spots = pl.pallas_call(
        middle_kernel,
        out_shape=(block,) * 5 + (struct(S_ROWS, BK), struct(S_ROWS, BK), struct(8, 3 * DMAX)),
        in_specs=[vmem] * 10,
        out_specs=(vmem,) * 8,
        input_output_aliases={n: n for n in range(5)},
        scratch_shapes=[pltpu.VMEM((6 * BJ + 16, BK), F32)],
        compiler_params=params,
        name="middle",
    )(*exts, pair_a, pair_b, pack_a, sums, info)
    stream_a = lax.ppermute(up_a, "stream", pairs(streams, 0, False))
    stream_b = lax.ppermute(up_b, "stream", pairs(streams, 1, False))

    outs = (struct(3, BI, BJ, BK), struct(BI, BJ, BK))
    *exts, done = pl.pallas_call(
        inner_kernel,
        out_shape=(block,) * 11 + (struct(4, INNER[1] - INNER[0], BJ, BK),),
        in_specs=[vmem] * 7,
        out_specs=(vmem,) * 12,
        input_output_aliases={n: n for n in range(5)},
        compiler_params=params,
        name="inner",
    )(*exts, spots, up_a)
    return tuple(
        pl.pallas_call(
            outer_kernel,
            out_shape=(block,) * 11 + outs,
            in_specs=[vmem] * 15,
            out_specs=(vmem,) * 11 + (hbm,) * 2,
            input_output_aliases={n: n for n in range(11)},
            scratch_shapes=[pltpu.VMEM((4, 8, BJ, BK), F32), pltpu.SemaphoreType.DMA((12,))],
            compiler_params=params,
            name="outer",
        )(*exts, stream_a, stream_b, info, done)[11:]
    )


def solution(mesh):
    block = P("stream", "girth", None)
    placed = (P(None, "stream", "girth", None), block, block, block, block, P("stream", "girth"), block, P("stream", "girth"))
    return jax.shard_map(
        body,
        mesh=mesh,
        in_specs=placed,
        out_specs=(P(None, "stream", "girth", None), block),
        check_vma=False,
    )
```

```python
import jax
import jax.numpy as jnp
from jax import lax
from jax.experimental import pallas as pl
from jax.experimental.pallas import tpu as pltpu
from jax.sharding import PartitionSpec as P

viscosity = 0.02
thrust = 8.0
target_speed = 0.5

BI, BJ, BK, DMAX = 32, 16, 128, 512
CELLS = BI * BJ
COLS = (3, 4, 3, 4, 3)
COL_AT = (0, 3, 7, 10, 14)
LAYERS = (4, 3, 3, 4, 3)
LAYER_AT = (0, 4, 7, 10, 14)
LIST_ROWS = 12
G_LIST = 17 * BI
G_ROWS = G_LIST + 16
FORCE_AT = 17
S_SIDE = 20 * BJ
S_FACE = 392
S_ROWS = S_FACE + 8
INNER = (8, 32)
EL, EC = BI + 8, 48
LO, LO_OUT, LO_IN, OWN, HI_IN, HI_OUT, HI = 10, 14, 15, 16, 32, 33, 34
F32, BF16, I32 = jnp.float32, jnp.bfloat16, jnp.int32


def iota(shape, dim):
    return lax.broadcasted_iota(I32, shape, dim)


def is_odd(axis):
    return lax.axis_index(axis) % 2 == 1


def by_parity(axis, even, odd):
    flag = is_odd(axis)
    pl.when(jnp.logical_not(flag))(even)
    pl.when(flag)(odd)


def three(x):
    a = x.astype(BF16)
    rest = x - a.astype(F32)
    b = rest.astype(BF16)
    c = (rest - b.astype(F32)).astype(BF16)
    return a, b, c


def side_rows(f):
    reach = (4, 4, 4, 4, 3, 3)
    depths = LAYERS + (3,)
    at = S_SIDE
    for g in range(f + 1):
        found = []
        for d in range(1, depths[g] + 1):
            width = reach[g] - d
            found.append((d, at, width))
            at += 2 * width
    return found


def wide_row(ref, at):
    return jnp.concatenate([ref[at + q : at + q + 1, :] for q in range(4)], axis=1)


def lines(ref):
    return ref.reshape(EL * EC, BK)


def put_row(ref, at, row):
    for q in range(4):
        ref[at + q : at + q + 1, :] = row[:, q * BK : (q + 1) * BK]


def head_kernel(vel, prs, tk, tw, cells, sector, weight, face, *refs):
    block, (sums, pack_a, pack_b, info) = refs[:5], refs[5:9]
    k_buf, w_buf, cell_buf, owner_buf, share_buf, face_buf, sem = refs[9:]
    inside = (slice(4, 4 + BI), slice(OWN, OWN + BJ))
    pairs = (
        (cells, cell_buf),
        (sector, owner_buf),
        (weight, share_buf),
        (face, face_buf),
        (vel.at[0], block[0].at[inside]),
        (vel.at[1], block[1].at[inside]),
        (vel.at[2], block[2].at[inside]),
        (prs, block[3].at[inside]),
        (tk, k_buf),
        (tw, w_buf),
    )
    copies = [pltpu.make_async_copy(a, b, sem.at[n]) for n, (a, b) in enumerate(pairs)]
    for copy in copies:
        copy.start()
    for copy in copies[:4]:
        copy.wait()
    cell, owner, share = cell_buf[...], owner_buf[...], share_buf[...]
    for ref in (pack_a, pack_b):
        put_row(ref, G_LIST, cell.astype(F32))
        put_row(ref, G_LIST + 4, owner.astype(F32))
        put_row(ref, G_LIST + 8, share)
        ref[G_LIST + LIST_ROWS : G_ROWS, :] = jnp.zeros((4, BK), F32)
    row = iota((8, BK), 0)
    sides = jnp.where(row == 0, face_buf[0, 0, 0], jnp.where(row == 1, face_buf[0, 0, 1], 0))
    info[...] = sides.astype(F32)
    pick = jnp.where(iota((CELLS, DMAX), 0) == cell // BK, 1.0, 0.0).astype(BF16)
    mine = iota((64, DMAX), 0)
    copies[4].wait()
    parts = jnp.concatenate(three(block[0][inside].reshape(CELLS, BK)), axis=1)
    found = lax.dot_general(parts, pick, (((0,), (0,)), ((), ())), preferred_element_type=F32)
    found = found[:BK] + found[BK : 2 * BK] + found[2 * BK :]
    inflow = jnp.sum(jnp.where(iota((BK, DMAX), 0) == cell % BK, found, 0.0), axis=0, keepdims=True)
    both = jnp.where(mine == owner, inflow, 0.0) + jnp.where(mine == owner + 32, 1.0, 0.0)
    both = jnp.concatenate([both, jnp.zeros((64, DMAX), F32)], axis=0)
    total = lax.dot_general(
        jnp.ones((8, DMAX), F32),
        both,
        (((1,), (1,)), ((), ())),
        precision=lax.Precision.HIGHEST,
        preferred_element_type=F32,
    )
    for t in range(sums.shape[0] // 8):
        sums[t * 8 : t * 8 + 8, :] = total
    def pack(to_high, to_low, fields):
        for f in fields:
            flat, n = lines(block[f]), COLS[f]
            for c in range(n):
                at = (COL_AT[f] + c) * BI
                to_high[at : at + BI, :] = flat[pl.ds(4 * EC + OWN + BJ - n + c, BI, stride=EC), :]
                to_low[at : at + BI, :] = flat[pl.ds(4 * EC + OWN + c, BI, stride=EC), :]

    for waited, fields in (((5, 6, 7), range(4)), ((8, 9), (4,))):
        for n in waited:
            copies[n].wait()
        if 4 in fields:
            block[4][inside] = viscosity + k_buf[...] / w_buf[...]
        by_parity("girth", lambda: pack(pack_a, pack_b, fields), lambda: pack(pack_b, pack_a, fields))


def listed(own, pair_a, pair_b):
    flag = is_odd("girth")
    rows = []
    for at in (G_LIST, G_LIST + 4, G_LIST + 8):
        a, b = wide_row(pair_a, at), wide_row(pair_b, at)
        rows.append(jnp.concatenate([wide_row(own, at), jnp.where(flag, a, b), jnp.where(flag, b, a)], axis=1))
    return rows[0].astype(I32), rows[1].astype(I32), rows[2]


def list_load(owner, share, load):
    mine = jnp.where(iota((32, owner.shape[1]), 0) == owner, 1.0, 0.0)
    given = jnp.dot(load[:, :32], mine, precision=lax.Precision.HIGHEST, preferred_element_type=F32)
    return given[:1] * share


def spread_rows(cell, given, row, count):
    size = cell.shape[1]
    here = jnp.where(iota((BK, size), 0) == cell % BK, 1.0, 0.0).astype(BF16)
    hit = iota((count, size), 0) == row
    picks = [jnp.where(hit, part.astype(F32), 0.0).astype(BF16) for part in three(given)]
    out = lax.dot_general(
        jnp.concatenate(picks, axis=0), here, (((1,), (1,)), ((), ())), preferred_element_type=F32
    )
    return out[:count] + out[count : 2 * count] + out[2 * count :]


def middle_kernel(*refs):
    (pair_a, pair_b, own_list, sums, info) = refs[5:10]
    block, (pack_b, pack_a, spots), (force,) = refs[10:15], refs[15:18], refs[18:]

    flag = is_odd("girth")
    for f in range(5):
        flat, m = lines(block[f]), COLS[f]
        for c in range(m):
            at = (COL_AT[f] + c) * BI
            a, b = pair_a[at : at + BI, :], pair_b[at : at + BI, :]
            flat[pl.ds(4 * EC + LO + 4 - m + c, BI, stride=EC), :] = jnp.where(flag, a, b)
            flat[pl.ds(4 * EC + HI + c, BI, stride=EC), :] = jnp.where(flag, b, a)
    total = jnp.sum(sums[...], axis=0, keepdims=True)
    filled = pltpu.roll(jnp.broadcast_to(total, (8, BK)), BK - 32, 1)[:1]
    value = thrust * (target_speed - total / jnp.maximum(filled, 1.0))
    value = jnp.broadcast_to(jnp.where(iota((1, BK), 1) < 32, value, 0.0), (8, BK))
    cell, owner, share = listed(own_list, pair_a, pair_b)
    given = list_load(owner, share, value)
    spots[0:1, :] = cell.astype(F32)
    spots[1:2, :] = given
    i, j = cell // (BJ * BK), (cell // BK) % BJ
    side = iota(cell.shape, 1) // DMAX
    edge = jnp.where(i < 3, i, jnp.where(i >= BI - 3, i - (BI - 6), -1))
    own_row = jnp.where(edge >= 0, edge * BJ + j, -1)
    corner = jnp.where(i < 2, i, jnp.where(i >= BI - 2, i - (BI - 4), -1))
    first = jnp.where(side == 1, BJ - 2, 0)
    across = j - first
    near = (corner >= 0) & (across >= 0) & (across < 2)
    side_row = jnp.where(near, 6 * BJ + (side - 1) * 8 + corner * 2 + across, -1)
    row = jnp.where(side == 0, own_row, side_row)
    force[...] = spread_rows(cell, given, row, 6 * BJ + 16)
    by_parity(
        "stream",
        lambda: stream_packs(block, force, info, pack_a, pack_b),
        lambda: stream_packs(block, force, info, pack_b, pack_a),
    )


def stream_packs(block, force, info, up, down):
    for f in range(5):
        n = LAYERS[f]
        for q in range(n):
            at = (LAYER_AT[f] + q) * BJ
            up[at : at + BJ, :] = block[f][4 + BI - n + q, OWN : OWN + BJ, :]
            down[at : at + BJ, :] = block[f][4 + q, OWN : OWN + BJ, :]
        for d, at, width in side_rows(f):
            if width:
                for ref, l in ((up, 4 + BI - d), (down, 3 + d)):
                    ref[at : at + width, :] = block[f][l, LO + 4 - width : LO + 4, :]
                    ref[at + width : at + 2 * width, :] = block[f][l, HI : HI + width, :]
    for q in range(3):
        at = (FORCE_AT + q) * BJ
        up[at : at + BJ, :] = force[(3 + q) * BJ : (4 + q) * BJ, :]
        down[at : at + BJ, :] = force[q * BJ : (q + 1) * BJ, :]
    for d, at, width in side_rows(5):
        if width:
            for ref, c in ((up, 4 - d), (down, d - 1)):
                low = 6 * BJ + 2 * c
                ref[at : at + width, :] = force[low + 2 - width : low + 2, :]
                ref[at + width : at + 2 * width, :] = force[low + 8 : low + 8 + width, :]
    for ref in (up, down):
        ref[S_FACE : S_FACE + 8, :] = info[...]


def images(ref, start, count, low_turned, high_turned, outer=True):
    flat = lines(ref)
    backward = BK - 1 - iota((count, BK), 1)
    for source, target, mask in (
        (LO + 3, LO_IN, low_turned),
        (HI, HI_IN, high_turned),
        (OWN, LO_OUT, low_turned),
        (OWN + BJ - 1, HI_OUT, high_turned),
    )[: 4 if outer else 2]:
        value = flat[pl.ds(start * EC + source, count, stride=EC), :]
        mirror = jnp.take_along_axis(value, backward, axis=1, mode="promise_in_bounds")
        flat[pl.ds(start * EC + target, count, stride=EC), :] = jnp.where(mask, mirror, value)


MID, LEFT, RIGHT = slice(8, 40), slice(7, 39), slice(9, 41)
NEAR, NEAR_LEFT, NEAR_RIGHT = slice(OWN, OWN + BJ), slice(OWN - 1, OWN + BJ - 1), slice(OWN + 1, OWN + BJ + 1)


def below(x, sign):
    return jnp.where(iota(x.shape, 1) == 0, sign * x, pltpu.roll(x, 1, 1))


def above(x):
    return jnp.where(iota(x.shape, 1) == BK - 1, 0.0, pltpu.roll(x, BK - 1, 1))


def star_layer(block, force, star, l):
    e = block[4][l, MID, :]
    share = 1.0 / (1.0 + 3.0 * e)
    half = 0.5 * e
    p = block[3]
    q = p[l, MID, :]
    slope = (
        p[l + 1, MID, :] - p[l - 1, MID, :],
        p[l, RIGHT, :] - p[l, LEFT, :],
        above(q) - below(q, 1.0),
    )
    for c in range(3):
        u = block[c]
        x, a, b = u[l, MID, :], u[l - 1, MID, :], u[l + 1, MID, :]
        around = a + b + u[l, LEFT, :] + u[l, RIGHT, :] + below(x, -1.0) + above(x)
        value = x - 0.125 * (b - a) + half * around - 0.25 * slope[c]
        if c == 0:
            value = value + 0.5 * force[l, MID, :]
        star[c][l, MID, :] = value * share


def sweep_layer(star, sweep, l):
    x = star[2][l, MID, :]
    total = (star[0][l + 1, MID, :] - star[0][l - 1, MID, :]) + (star[1][l, RIGHT, :] - star[1][l, LEFT, :])
    sweep[l, MID, :] = (total + (above(x) - below(x, -1.0))) * (-1.0 / 6.0)


def second_layer(sweep, second, l):
    x = sweep[l, MID, :]
    around = sweep[l - 1, MID, :] + sweep[l + 1, MID, :] + sweep[l, LEFT, :] + sweep[l, RIGHT, :]
    second[l, MID, :] = (around + below(x, 1.0) + above(x)) * (1.0 / 6.0) + x


def out_layer(block, star, second, stage, l, at):
    x = second[l, NEAR, :]
    slope = (
        second[l + 1, NEAR, :] - second[l - 1, NEAR, :],
        second[l, NEAR_RIGHT, :] - second[l, NEAR_LEFT, :],
        above(x) - below(x, 1.0),
    )
    for c in range(3):
        stage[c, at] = star[c][l, NEAR, :] - 0.25 * slope[c]
    stage[3, at] = block[3][l, NEAR, :] + x


def layers(start, stop, step, unroll):
    def run(l, carry):
        step(l)
        return carry

    lax.fori_loop(start, stop, run, 0, unroll=unroll)


def inner_kernel(*refs):
    spots, info = refs[5], refs[6].at[S_FACE : S_FACE + 8, :]
    block, star, (force, sweep, second) = refs[7:12], refs[12:15], refs[15:18]
    stage = refs[18]
    cell, given = spots[0:1, :].astype(I32), spots[1:2, :]
    i, j = cell // (BJ * BK), (cell // BK) % BJ
    own, low, high = (slice(n * DMAX, (n + 1) * DMAX) for n in range(3))
    out = spread_rows(cell[:, own], given[:, own], cell[:, own] // BK, CELLS)
    force[4 : 4 + BI, NEAR, :] = out.reshape(BI, BJ, BK)
    flat = lines(force)
    for part, j0, at in ((low, BJ - 2, LO + 2), (high, 0, HI)):
        across = j[:, part] - j0
        row = jnp.where((across >= 0) & (across < 2), across * BI + i[:, part], -1)
        out = spread_rows(cell[:, part], given[:, part], row, 2 * BI)
        for c in range(2):
            flat[pl.ds(4 * EC + at + c, BI, stride=EC), :] = out[c * BI : (c + 1) * BI]
    low_turned, high_turned = info[0:1, :] > 0.5, info[1:2, :] > 0.5
    a, b = INNER
    for f in range(4):
        images(block[f], 4, BI, low_turned, high_turned)
    layers(a - 3, b + 3, lambda l: star_layer(block, force, star, l), 15)
    images(star[1], a - 3, b - a + 6, low_turned, high_turned)
    layers(a - 2, b + 2, lambda l: sweep_layer(star, sweep, l), 28)
    images(sweep, a - 2, b - a + 4, low_turned, high_turned)
    layers(a - 1, b + 1, lambda l: second_layer(sweep, second, l), 26)
    images(second, a - 1, b - a + 2, low_turned, high_turned, outer=False)
    layers(a, b, lambda l: out_layer(block, star, second, stage, l, l - a), 8)


def outer_kernel(*refs):
    pair_a, pair_b, info, done = refs[11:15]
    refs = refs[15:]
    block, star, (force, sweep, second) = refs[:5], refs[5:8], refs[8:11]
    vel_out, prs_out, stage, sem = refs[11:]
    a, b = INNER
    inside = slice(a - 4, b - 4)
    copies = [pltpu.make_async_copy(done.at[c], vel_out.at[c, inside], sem.at[8 + c]) for c in range(3)]
    copies.append(pltpu.make_async_copy(done.at[3], prs_out.at[inside], sem.at[11]))
    for copy in copies:
        copy.start()
    place = lax.axis_index("stream")
    first_row = place == 0
    last_row = place == lax.axis_size("stream") - 1

    flag = is_odd("stream")

    def arrived(at, count):
        a, b = pair_a[at : at + count, :], pair_b[at : at + count, :]
        return jnp.where(flag, a, b), jnp.where(flag, b, a)

    for f in range(6):
        to, n, base = (block[f], LAYERS[f], LAYER_AT[f]) if f < 5 else (force, 3, FORCE_AT)
        for q in range(n):
            up, down = arrived((base + q) * BJ, BJ)
            to[4 - n + q, OWN : OWN + BJ, :] = up
            to[4 + BI + q, OWN : OWN + BJ, :] = down
        for d, at, width in side_rows(f):
            if width:
                for side, start in ((LO + 4 - width, at), (HI, at + width)):
                    up, down = arrived(start, width)
                    to[4 - d, side : side + width, :] = up
                    to[3 + BI + d, side : side + width, :] = down
    face_a, face_b = pair_a[S_FACE : S_FACE + 8, :], pair_b[S_FACE : S_FACE + 8, :]
    up_face, down_face = jnp.where(flag, face_a, face_b), jnp.where(flag, face_b, face_a)

    def both(ref, down, outer=True):
        for start, other in ((down, up_face), (EL - 4 - down, down_face)):
            l = iota((4, BK), 0) + start
            here = (l >= 4) & (l < 4 + BI)
            low = jnp.where(here, info[0:1, :], other[0:1, :]) > 0.5
            high = jnp.where(here, info[1:2, :], other[1:2, :]) > 0.5
            images(ref, start, 4, low, high, outer)

    def ends(down, step):
        for l in (*range(down, down + 4), *range(EL - 4 - down, EL - down)):
            step(l)

    def edges(ref, low, high):
        ref[3, MID, :] = jnp.where(first_row, low, ref[3, MID, :])
        ref[4 + BI, MID, :] = jnp.where(last_row, high, ref[4 + BI, MID, :])

    for ref in block[:3]:
        edges(ref, 0.0, ref[3 + BI, MID, :])
    edges(block[3], block[3][4, MID, :], 0.0)
    for f in range(4):
        both(block[f], 0)
    ends(1, lambda l: star_layer(block, force, star, l))

    edges(star[0], 0.0, star[0][3 + BI, MID, :])
    both(star[1], 1)
    ends(2, lambda l: sweep_layer(star, sweep, l))

    edges(sweep, sweep[4, MID, :], 0.0)
    both(sweep, 2)
    ends(3, lambda l: second_layer(sweep, second, l))

    edges(second, second[4, MID, :], 0.0)
    both(second, 4, outer=False)
    for start in (4, b):
        at = 0 if start == 4 else 4
        for q in range(4):
            out_layer(block, star, second, stage, start + q, at + q)
        part, to = slice(at, at + 4), slice(start - 4, start)
        for c in range(3):
            copies.append(pltpu.make_async_copy(stage.at[c, part], vel_out.at[c, to], sem.at[at + c]))
        copies.append(pltpu.make_async_copy(stage.at[3, part], prs_out.at[to], sem.at[at + 3]))
        for copy in copies[at + 4 :]:
            copy.start()
    for copy in copies:
        copy.wait()


def body(velocity, pressure, turb_k, turb_omega, face_code, disc_cells, disc_sector, disc_weight):
    streams, girths = lax.axis_size("stream"), lax.axis_size("girth")
    vmem = pl.BlockSpec(memory_space=pltpu.VMEM)
    hbm = pl.BlockSpec(memory_space=pltpu.HBM)
    params = pltpu.CompilerParams(vmem_limit_bytes=24 * 2**20)

    def struct(*shape):
        return jax.ShapeDtypeStruct(shape, F32)

    block = struct(EL, EC, BK)
    fields = (velocity, pressure, turb_k, turb_omega, disc_cells, disc_sector.reshape(1, DMAX), disc_weight, face_code)
    *exts, sums, pack_a, pack_b, info = pl.pallas_call(
        head_kernel,
        out_shape=(block,) * 5 + (struct(girths, BK), struct(G_ROWS, BK), struct(G_ROWS, BK), struct(8, BK)),
        in_specs=[hbm] * 8,
        out_specs=(vmem,) * 9,
        scratch_shapes=[
            pltpu.VMEM((BI, BJ, BK), F32),
            pltpu.VMEM((BI, BJ, BK), F32),
            pltpu.VMEM((1, DMAX), I32),
            pltpu.VMEM((1, DMAX), I32),
            pltpu.VMEM((1, DMAX), F32),
            pltpu.SMEM((1, 1, 2), I32),
            pltpu.SemaphoreType.DMA((10,)),
        ],
        compiler_params=params,
        name="head",
    )(*(pltpu.with_memory_space_constraint(x, pltpu.HBM) for x in fields))

    def pairs(size, first, cyclic):
        ends = [(n, (n + 1) % size) for n in range(first, size, 2) if cyclic or n + 1 < size]
        return [pair for a, b in ends for pair in ((a, b), (b, a))]

    pair_b = lax.ppermute(pack_b, "girth", pairs(girths, 1, True))
    pair_a = lax.ppermute(pack_a, "girth", pairs(girths, 0, True))
    sums = lax.all_to_all(sums, "girth", split_axis=0, concat_axis=0, tiled=True)

    *exts, up_b, up_a, spots = pl.pallas_call(
        middle_kernel,
        out_shape=(block,) * 5 + (struct(S_ROWS, BK), struct(S_ROWS, BK), struct(8, 3 * DMAX)),
        in_specs=[vmem] * 10,
        out_specs=(vmem,) * 8,
        input_output_aliases={n: n for n in range(5)},
        scratch_shapes=[pltpu.VMEM((6 * BJ + 16, BK), F32)],
        compiler_params=params,
        name="middle",
    )(*exts, pair_a, pair_b, pack_a, sums, info)
    stream_a = lax.ppermute(up_a, "stream", pairs(streams, 0, False))
    stream_b = lax.ppermute(up_b, "stream", pairs(streams, 1, False))

    outs = (struct(3, BI, BJ, BK), struct(BI, BJ, BK))
    *exts, done = pl.pallas_call(
        inner_kernel,
        out_shape=(block,) * 11 + (struct(4, INNER[1] - INNER[0], BJ, BK),),
        in_specs=[vmem] * 7,
        out_specs=(vmem,) * 12,
        input_output_aliases={n: n for n in range(5)},
        compiler_params=params,
        name="inner",
    )(*exts, spots, up_a)
    return tuple(
        pl.pallas_call(
            outer_kernel,
            out_shape=(block,) * 11 + outs,
            in_specs=[vmem] * 15,
            out_specs=(vmem,) * 11 + (hbm,) * 2,
            input_output_aliases={n: n for n in range(11)},
            scratch_shapes=[pltpu.VMEM((4, 8, BJ, BK), F32), pltpu.SemaphoreType.DMA((12,))],
            compiler_params=params,
            name="outer",
        )(*exts, stream_a, stream_b, info, done)[11:]
    )


def solution(mesh):
    block = P("stream", "girth", None)
    placed = (P(None, "stream", "girth", None), block, block, block, block, P("stream", "girth"), block, P("stream", "girth"))
    return jax.shard_map(
        body,
        mesh=mesh,
        in_specs=placed,
        out_specs=(P(None, "stream", "girth", None), block),
        check_vma=False,
    )
```
